32 devices in a mesh: dp: 8 (over z, x), seq: 4 (over y, core).
Axes of the slice: x: 2, y: 2, z: 4, core: 2. Of those that a mesh axis runs over, the one named last changes fastest.
Arguments:
- layer_in: bfloat16 [16, 256, 768], P('dp', 'seq'), may hold values from -6 to 6
- lengths: int32 [16], P('dp'), may hold values from 64 to 256, as said below
- qkv_weight: bfloat16 [768, 2304], P('dp'), may hold values from -6 to 6
- query_bias: bfloat16 [768], P('dp'), may hold values from -3 to 3
- value_bias: bfloat16 [768], P('dp'), may hold values from -3 to 3
- out_weight: bfloat16 [768, 768], P('dp'), may hold values from -2.5 to 2.5
- out_bias: bfloat16 [768], P('dp'), may hold values from -3 to 3
- attn_gain: bfloat16 [768], P('dp'), may hold values from 0.099609375 to 1.8984375
- attn_shift: bfloat16 [768], P('dp'), may hold values from -3 to 3
- up_weight: bfloat16 [768, 3072], P('dp'), may hold values from -0.21875 to 0.21875
- up_bias: bfloat16 [3072], P('dp'), may hold values from -3 to 3
- down_weight: bfloat16 [3072, 768], P('dp'), may hold values from -0.109375 to 0.109375
- down_bias: bfloat16 [768], P('dp'), may hold values from -3 to 3
- ffn_gain: bfloat16 [768], P('dp'), may hold values from 0.099609375 to 1.8984375
- ffn_shift: bfloat16 [768], P('dp'), may hold values from -3 to 3
- grad_out: bfloat16 [16, 256, 768], P('dp', 'seq'), may hold values from -6 to 6
Outputs:
- layer_out: float32 [16, 256, 768], P('dp', 'seq')
- grad_in: float32 [16, 256, 768], P('dp', 'seq')
- qkv_weight_grad: float32 [768, 2304], P('dp')
- query_bias_grad: float32 [768], P('dp')
- value_bias_grad: float32 [768], P('dp')
- out_weight_grad: float32 [768, 768], P('dp')
- out_bias_grad: float32 [768], P('dp')
- attn_gain_grad: float32 [768], P('dp')
- attn_shift_grad: float32 [768], P('dp')
- up_weight_grad: float32 [768, 3072], P('dp')
- up_bias_grad: float32 [3072], P('dp')
- down_weight_grad: float32 [3072, 768], P('dp')
- down_bias_grad: float32 [768], P('dp')
- ffn_gain_grad: float32 [768], P('dp')
- ffn_shift_grad: float32 [768], P('dp')
The draws below stay inside these ranges and needn't reach their ends.
Inputs may be any that keep to these rules, and one draw needn't show every extreme that they name: `lengths`: each sequence holds at least 64 real tokens at its start; keys at positions from its length on are padding that no query attends to; in every draw some sequence is 256 long.
All inputs are finite; a program needn't handle non-finite values.
Results may differ from the reference program's by a relative error of at most 0.012.
The reference program's roundings to bfloat16 on the way count: a program that leaves them out, or rounds other values in their place, can miss the bound.
Values may be sent and summed in bfloat16 or wider, within the bound.
A program may use at most 128 MiB of HBM per device.

```python
import math
import jax
import jax.numpy as jnp
from jax import lax

D = 768
H = 12
FF = 3072
HD = 64
LEN = 256
SEQS = 16


def draw_lengths(key, part):
    draw_key, pick_key = jax.random.split(jax.random.fold_in(key, 11))
    drawn = jax.random.randint(draw_key, (SEQS,), LEN // 4, LEN + 1)
    longest = jax.random.randint(pick_key, (), 0, SEQS)
    return jnp.where(jnp.arange(SEQS) == longest, LEN, drawn).astype(jnp.int32)


def draw_qkv_weight(key, part):
    noise_key = jax.random.fold_in(key, 23)
    base = jnp.clip(jax.random.normal(noise_key, (D, 3 * D), jnp.float32), -5.0, 5.0)
    return (base * D ** (-0.5)).astype(jnp.bfloat16)


def levels(stream_key, extent, shards, low, high):
    loudness = 1.0
    for axis_at, parts in shards:
        heights = jax.random.uniform(jax.random.fold_in(jax.random.fold_in(stream_key, 6), axis_at), (parts,), jnp.float32, low / len(shards), high / len(shards))
        loudness = loudness * jnp.repeat(jnp.exp(heights), extent[axis_at] // parts).reshape((-1,) + (1,) * (len(extent) - 1 - axis_at))
    return loudness


def scatter_about(stream_key, extent, scale, bound, cuts=(), dtype=jnp.bfloat16):
    level = levels(stream_key, extent, cuts, -0.22, 0.18) if cuts else 1.0
    values = jax.random.normal(stream_key, extent, jnp.float32) * scale * level
    return jnp.minimum(jnp.maximum(values, -bound), bound).astype(dtype)


def setup_inputs(seed: int = 0) -> dict:
    arg_keys = jax.random.split(jax.random.key(seed), 17)
    layer_in = scatter_about(arg_keys[0], (SEQS, LEN, D), 1.0, 6.0, ((0, 8), (1, 4)))
    lengths = draw_lengths(jax.random.fold_in(arg_keys[16], 71), 0)
    qkv_weight = draw_qkv_weight(jax.random.fold_in(arg_keys[16], 71), 0)
    query_bias = scatter_about(arg_keys[3], (D,), 0.5, 3.0, ((0, 8),))
    value_bias = scatter_about(arg_keys[4], (D,), 0.5, 3.0, ((0, 8),))
    out_weight = scatter_about(arg_keys[5], (D, D), (max(1, 2 * D // LEN)) ** -0.5, 2.5, ((0, 8),))
    out_bias = scatter_about(arg_keys[6], (D,), 0.5, 3.0, ((0, 8),))
    attn_gain = jnp.clip(1.0 + 0.18 * jax.random.normal(arg_keys[7], (D,), jnp.float32), 0.099609375, 1.8984375).astype(jnp.bfloat16)
    attn_shift = scatter_about(arg_keys[8], (D,), 0.5, 3.0, ((0, 8),))
    up_weight = scatter_about(arg_keys[9], (D, FF), D ** -0.5, 0.21875, ((0, 8),))
    up_bias = scatter_about(arg_keys[10], (FF,), 0.5, 3.0, ((0, 8),))
    down_weight = scatter_about(arg_keys[11], (FF, D), FF ** -0.5, 0.109375, ((0, 8),))
    down_bias = scatter_about(arg_keys[12], (D,), 0.5, 3.0, ((0, 8),))
    ffn_gain = jnp.clip(1.0 + 0.18 * jax.random.normal(arg_keys[13], (D,), jnp.float32), 0.099609375, 1.8984375).astype(jnp.bfloat16)
    ffn_shift = scatter_about(arg_keys[14], (D,), 0.5, 3.0, ((0, 8),))
    grad_out = scatter_about(arg_keys[15], (SEQS, LEN, D), 1.0, 6.0, ((0, 8), (1, 4)))
    return dict(layer_in=layer_in, lengths=lengths, qkv_weight=qkv_weight, query_bias=query_bias, value_bias=value_bias, out_weight=out_weight, out_bias=out_bias, attn_gain=attn_gain, attn_shift=attn_shift, up_weight=up_weight, up_bias=up_bias, down_weight=down_weight, down_bias=down_bias, ffn_gain=ffn_gain, ffn_shift=ffn_shift, grad_out=grad_out)


norm_eps = 1e-12
mask_fill = -1e+30

def layer_norm(hidden, gain, shift):
    centred = hidden - lax.optimization_barrier(jnp.mean(hidden, axis=-1, keepdims=True))
    inverse = lax.rsqrt(lax.optimization_barrier(jnp.mean(centred * centred, axis=-1, keepdims=True)) + norm_eps)
    normed = centred * inverse
    return (normed * gain + shift, normed, inverse)

def norm_back(grad_norm, normed, inverse, gain):
    scaled = grad_norm * gain
    middle = scaled - lax.optimization_barrier(jnp.mean(scaled, axis=-1, keepdims=True))
    return inverse * (middle - normed * lax.optimization_barrier(jnp.mean(scaled * normed, axis=-1, keepdims=True)))

def gelu_exact(inner):
    return 0.5 * inner * (1.0 + jax.scipy.special.erf(inner * (1.0 / math.sqrt(2.0))))

def gelu_slope(inner):
    cumul = 0.5 * (1.0 + jax.scipy.special.erf(inner * (1.0 / math.sqrt(2.0))))
    return cumul + inner * jnp.exp(-0.5 * inner * inner) * (1.0 / math.sqrt(2.0 * math.pi))

def widened(array):
    return lax.optimization_barrier(array.astype(jnp.bfloat16)).astype(jnp.float32)

def reference(layer_in, lengths, qkv_weight, query_bias, value_bias, out_weight, out_bias, attn_gain, attn_shift, up_weight, up_bias, down_weight, down_bias, ffn_gain, ffn_shift, grad_out):
    params = (qkv_weight, query_bias, value_bias, out_weight, out_bias, attn_gain, attn_shift, up_weight, up_bias, down_weight, down_bias, ffn_gain, ffn_shift)
    score_scale = HD ** (-0.5)
    bias_qkv = jnp.concatenate([query_bias.astype(jnp.float32), jnp.zeros((D,), jnp.float32), value_bias.astype(jnp.float32)])
    out_shift = out_bias.astype(jnp.float32)
    gain_one = attn_gain.astype(jnp.float32)
    shift_one = attn_shift.astype(jnp.float32)
    up_shift = up_bias.astype(jnp.float32)
    down_shift = down_bias.astype(jnp.float32)
    gain_two = ffn_gain.astype(jnp.float32)
    shift_two = ffn_shift.astype(jnp.float32)
    positions = jnp.arange(LEN).astype(jnp.int32)

    def one_sequence(totals, item):
        tokens, length, cotangent = item
        rows_in = tokens.astype(jnp.float32)
        qkv_proj = widened(jnp.dot(tokens, qkv_weight, preferred_element_type=jnp.float32) + bias_qkv)
        split = qkv_proj.reshape(LEN, 3, H, HD)
        queries = split[:, 0]
        keys = split[:, 1]
        values = split[:, 2]
        valid = positions < length.astype(jnp.int32)
        scores = jnp.einsum('qhd,khd->hqk', queries, keys) * score_scale
        scores = jnp.where(valid[None, None, :], scores, mask_fill)
        row_top = lax.optimization_barrier(jnp.max(scores, axis=-1, keepdims=True))
        log_sum = row_top + jnp.log(lax.optimization_barrier(jnp.sum(jnp.exp(scores - row_top), axis=-1, keepdims=True)))
        probs_exact = jnp.exp(scores - log_sum)
        probs = widened(probs_exact)
        attended = jnp.einsum('hqk,khd->qhd', probs, values).reshape(LEN, D).astype(jnp.bfloat16)
        first_sum = rows_in + jnp.dot(attended, out_weight, preferred_element_type=jnp.float32) + out_shift
        first_norm, normed_one, inverse_one = layer_norm(first_sum, gain_one, shift_one)
        first_round = first_norm.astype(jnp.bfloat16)
        inner = jnp.dot(first_round, up_weight, preferred_element_type=jnp.float32) + up_shift
        activated = gelu_exact(inner).astype(jnp.bfloat16)
        second_sum = first_norm + jnp.dot(activated, down_weight, preferred_element_type=jnp.float32) + down_shift
        layer_out, normed_two, inverse_two = layer_norm(second_sum, gain_two, shift_two)
        upstream = cotangent.astype(jnp.float32)
        ffn_gain_grad = lax.optimization_barrier(jnp.sum(upstream * normed_two, axis=0))
        ffn_shift_grad = lax.optimization_barrier(jnp.sum(upstream, axis=0))
        d_second = norm_back(upstream, normed_two, inverse_two, gain_two)
        d_second_round = d_second.astype(jnp.bfloat16)
        down_weight_grad = jnp.dot(activated.T, d_second_round, preferred_element_type=jnp.float32)
        down_bias_grad = lax.optimization_barrier(jnp.sum(d_second, axis=0))
        d_inner = jnp.dot(d_second_round, down_weight.T, preferred_element_type=jnp.float32) * gelu_slope(inner)
        d_inner_round = d_inner.astype(jnp.bfloat16)
        up_weight_grad = jnp.dot(first_round.T, d_inner_round, preferred_element_type=jnp.float32)
        up_bias_grad = lax.optimization_barrier(jnp.sum(d_inner, axis=0))
        d_first_norm = d_second + jnp.dot(d_inner_round, up_weight.T, preferred_element_type=jnp.float32)
        attn_gain_grad = lax.optimization_barrier(jnp.sum(d_first_norm * normed_one, axis=0))
        attn_shift_grad = lax.optimization_barrier(jnp.sum(d_first_norm, axis=0))
        d_first = norm_back(d_first_norm, normed_one, inverse_one, gain_one)
        d_first_round = d_first.astype(jnp.bfloat16)
        out_weight_grad = jnp.dot(attended.T, d_first_round, preferred_element_type=jnp.float32)
        out_bias_grad = lax.optimization_barrier(jnp.sum(d_first, axis=0))
        d_attended = widened(jnp.dot(d_first_round, out_weight.T, preferred_element_type=jnp.float32)).reshape(LEN, H, HD)
        d_probs = jnp.einsum('qhd,khd->hqk', d_attended, values)
        row_dot = lax.optimization_barrier(jnp.sum(probs_exact * d_probs, axis=-1, keepdims=True))
        d_scores = widened(probs_exact * (d_probs - row_dot) * score_scale)
        d_query = jnp.einsum('hqk,khd->qhd', d_scores, keys).reshape(LEN, D)
        d_key = jnp.einsum('hqk,qhd->khd', d_scores, queries).reshape(LEN, D)
        d_value = jnp.einsum('hqk,qhd->khd', probs, d_attended).reshape(LEN, D)
        d_qkv = jnp.concatenate([d_query, d_key, d_value], axis=1).astype(jnp.bfloat16)
        qkv_weight_grad = jnp.dot(tokens.T, d_qkv, preferred_element_type=jnp.float32)
        query_bias_grad = lax.optimization_barrier(jnp.sum(d_query, axis=0))
        value_bias_grad = lax.optimization_barrier(jnp.sum(d_value, axis=0))
        grad_in = d_first + jnp.dot(d_qkv, qkv_weight.T, preferred_element_type=jnp.float32)
        step_grads = (qkv_weight_grad, query_bias_grad, value_bias_grad, out_weight_grad, out_bias_grad, attn_gain_grad, attn_shift_grad, up_weight_grad, up_bias_grad, down_weight_grad, down_bias_grad, ffn_gain_grad, ffn_shift_grad)
        return (jax.tree.map(jnp.add, totals, step_grads), (layer_out, grad_in))
    start = tuple((jnp.zeros(param.shape, jnp.float32) for param in params))
    totals, stacked = lax.scan(one_sequence, start, (layer_in, lengths, grad_out))
    layer_out, grad_in = stacked
    return (layer_out, grad_in, totals[0], totals[1], totals[2], totals[3], totals[4], totals[5], totals[6], totals[7], totals[8], totals[9], totals[10], totals[11], totals[12])
```

```python
import math

import jax
import jax.numpy as jnp
from jax import lax
from jax.sharding import PartitionSpec as P

D = 768
H = 12
HD = 64
FF = 3072


norm_eps = 1e-12
mask_fill = -1e30


def layer_norm(hidden, gain, shift):
    centred = hidden - jnp.mean(hidden, axis=-1, keepdims=True)
    inverse = lax.rsqrt(jnp.mean(centred * centred, axis=-1, keepdims=True) + norm_eps)
    normed = centred * inverse
    return (normed * gain + shift, normed, inverse)


def norm_back(grad_norm, normed, inverse, gain):
    scaled = grad_norm * gain
    middle = scaled - jnp.mean(scaled, axis=-1, keepdims=True)
    return inverse * (middle - normed * jnp.mean(scaled * normed, axis=-1, keepdims=True))


def gelu_exact(inner):
    return 0.5 * inner * (1.0 + jax.scipy.special.erf(inner * (1.0 / math.sqrt(2.0))))


def gelu_slope(inner):
    cumul = 0.5 * (1.0 + jax.scipy.special.erf(inner * (1.0 / math.sqrt(2.0))))
    return cumul + inner * jnp.exp(-0.5 * inner * inner) * (1.0 / math.sqrt(2.0 * math.pi))


def on_device_general(
    layer_in,
    lengths,
    qkv_weight,
    query_bias,
    value_bias,
    out_weight,
    out_bias,
    attn_gain,
    attn_shift,
    up_weight,
    up_bias,
    down_weight,
    down_bias,
    ffn_gain,
    ffn_shift,
    grad_out,
):
    params = (
        qkv_weight,
        query_bias,
        value_bias,
        out_weight,
        out_bias,
        attn_gain,
        attn_shift,
        up_weight,
        up_bias,
        down_weight,
        down_bias,
        ffn_gain,
        ffn_shift,
    )
    gathered = (
        lax.all_gather(params[0], "dp", axis=0, tiled=True),
        lax.all_gather(params[1], "dp", axis=0, tiled=True),
        lax.all_gather(params[2], "dp", axis=0, tiled=True),
        lax.all_gather(params[3], "dp", axis=0, tiled=True),
        lax.all_gather(params[4], "dp", axis=0, tiled=True),
        lax.all_gather(params[5], "dp", axis=0, tiled=True),
        lax.all_gather(params[6], "dp", axis=0, tiled=True),
        lax.all_gather(params[7], "dp", axis=0, tiled=True),
        lax.all_gather(params[8], "dp", axis=0, tiled=True),
        lax.all_gather(params[9], "dp", axis=0, tiled=True),
        lax.all_gather(params[10], "dp", axis=0, tiled=True),
        lax.all_gather(params[11], "dp", axis=0, tiled=True),
        lax.all_gather(params[12], "dp", axis=0, tiled=True),
    )
    (
        w_qkv,
        q_bias,
        v_bias,
        w_out,
        b_out,
        gain_raw,
        shift_raw,
        w_up,
        b_up,
        w_down,
        b_down,
        gain_last,
        shift_last,
    ) = gathered
    seqs_here, block, width_model = layer_in.shape
    full_len = block * lax.axis_size("seq")
    rows = seqs_here * block
    pair_width = 2 * HD
    pair_count = H // 2
    score_scale = HD ** (-0.5)
    bias_qkv = jnp.concatenate(
        [q_bias.astype(jnp.float32), jnp.zeros((D,), jnp.float32), v_bias.astype(jnp.float32)]
    )
    gain_one = gain_raw.astype(jnp.float32)
    shift_one = shift_raw.astype(jnp.float32)
    gain_two = gain_last.astype(jnp.float32)
    shift_two = shift_last.astype(jnp.float32)
    tokens = layer_in.reshape(rows, D)
    qkv_proj = (jnp.dot(tokens, w_qkv, preferred_element_type=jnp.float32) + bias_qkv).astype(
        jnp.bfloat16
    )
    qkv_proj = qkv_proj.reshape(seqs_here, block, 3 * D)
    queries = qkv_proj[:, :, :D]
    keys_here = qkv_proj[:, :, D : 2 * D]
    values_here = qkv_proj[:, :, 2 * D :]
    keys_all, values_all = (
        lax.all_gather(keys_here, "seq", axis=1, tiled=True),
        lax.all_gather(values_here, "seq", axis=1, tiled=True),
    )
    valid = jnp.arange(full_len)[None, :] < lengths[:, None]

    def pair_part(array, pair_idx):
        piece = lax.dynamic_slice_in_dim(array, pair_idx * pair_width, pair_width, 2)
        return piece.reshape(piece.shape[:2] + (2, HD))

    def pair_scores(query_pair, key_pair):
        scores = (
            jnp.einsum("sbhd,slhd->shbl", query_pair, key_pair, preferred_element_type=jnp.float32)
            * score_scale
        )
        return jnp.where(valid[:, None, None, :], scores, mask_fill)

    def forward_pair(pair_idx):
        query_pair = pair_part(queries, pair_idx)
        key_pair = pair_part(keys_all, pair_idx)
        value_pair = pair_part(values_all, pair_idx)
        scores = pair_scores(query_pair, key_pair)
        row_top = jnp.max(scores, axis=-1, keepdims=True)
        log_sum = row_top + jnp.log(jnp.sum(jnp.exp(scores - row_top), axis=-1, keepdims=True))
        probs = jnp.exp(scores - log_sum).astype(jnp.bfloat16)
        mixed = jnp.einsum("shbl,slhd->sbhd", probs, value_pair, preferred_element_type=jnp.float32)
        return (mixed.astype(jnp.bfloat16).reshape(seqs_here, block, pair_width), log_sum)

    pair_out, log_sums = lax.map(forward_pair, jnp.arange(pair_count))

    def heads_side(stacked):
        return jnp.transpose(stacked, (1, 2, 0, 3)).reshape(rows, D)

    attended = heads_side(pair_out)
    first_sum = (
        tokens.astype(jnp.float32)
        + jnp.dot(attended, w_out, preferred_element_type=jnp.float32)
        + b_out.astype(jnp.float32)
    )
    first_norm, normed_one, inverse_one = layer_norm(first_sum, gain_one, shift_one)
    first_round = first_norm.astype(jnp.bfloat16)
    inner = jnp.dot(first_round, w_up, preferred_element_type=jnp.float32) + b_up.astype(
        jnp.float32
    )
    activated = gelu_exact(inner).astype(jnp.bfloat16)
    second_sum = (
        first_norm
        + jnp.dot(activated, w_down, preferred_element_type=jnp.float32)
        + b_down.astype(jnp.float32)
    )
    layer_out, normed_two, inverse_two = layer_norm(second_sum, gain_two, shift_two)
    (
        w_qkv,
        q_bias,
        v_bias,
        w_out,
        b_out,
        gain_raw,
        shift_raw,
        w_up,
        b_up,
        w_down,
        b_down,
        gain_last,
        shift_last,
    ) = (
        lax.all_gather(params[0], "dp", axis=0, tiled=True),
        lax.all_gather(params[1], "dp", axis=0, tiled=True),
        lax.all_gather(params[2], "dp", axis=0, tiled=True),
        lax.all_gather(params[3], "dp", axis=0, tiled=True),
        lax.all_gather(params[4], "dp", axis=0, tiled=True),
        lax.all_gather(params[5], "dp", axis=0, tiled=True),
        lax.all_gather(params[6], "dp", axis=0, tiled=True),
        lax.all_gather(params[7], "dp", axis=0, tiled=True),
        lax.all_gather(params[8], "dp", axis=0, tiled=True),
        lax.all_gather(params[9], "dp", axis=0, tiled=True),
        lax.all_gather(params[10], "dp", axis=0, tiled=True),
        lax.all_gather(params[11], "dp", axis=0, tiled=True),
        lax.all_gather(params[12], "dp", axis=0, tiled=True),
    )
    gain_one = gain_raw.astype(jnp.float32)
    gain_two = gain_last.astype(jnp.float32)
    upstream = grad_out.reshape(rows, D).astype(jnp.float32)
    ffn_gain_grad = jnp.sum(upstream * normed_two, axis=0)
    ffn_shift_grad = jnp.sum(upstream, axis=0)
    d_second = norm_back(upstream, normed_two, inverse_two, gain_two)
    d_second_round = d_second.astype(jnp.bfloat16)
    down_weight_grad = jnp.dot(activated.T, d_second_round, preferred_element_type=jnp.float32)
    down_bias_grad = jnp.sum(d_second, axis=0)
    d_inner = jnp.dot(d_second_round, w_down.T, preferred_element_type=jnp.float32) * gelu_slope(
        inner
    )
    d_inner_round = d_inner.astype(jnp.bfloat16)
    up_weight_grad = jnp.dot(first_round.T, d_inner_round, preferred_element_type=jnp.float32)
    up_bias_grad = jnp.sum(d_inner, axis=0)
    d_first_norm = d_second + jnp.dot(d_inner_round, w_up.T, preferred_element_type=jnp.float32)
    attn_gain_grad = jnp.sum(d_first_norm * normed_one, axis=0)
    attn_shift_grad = jnp.sum(d_first_norm, axis=0)
    d_first = norm_back(d_first_norm, normed_one, inverse_one, gain_one)
    d_first_round = d_first.astype(jnp.bfloat16)
    out_weight_grad = jnp.dot(attended.T, d_first_round, preferred_element_type=jnp.float32)
    out_bias_grad = jnp.sum(d_first, axis=0)
    d_attended = jnp.dot(d_first_round, w_out.T, preferred_element_type=jnp.float32).astype(
        jnp.bfloat16
    )
    d_attended = d_attended.reshape(seqs_here, block, D)

    def backward_pair(item):
        pair_idx, log_sum = item
        query_pair = pair_part(queries, pair_idx)
        key_pair = pair_part(keys_all, pair_idx)
        value_pair = pair_part(values_all, pair_idx)
        grad_pair = pair_part(d_attended, pair_idx)
        probs_exact = jnp.exp(pair_scores(query_pair, key_pair) - log_sum)
        d_probs = jnp.einsum(
            "sbhd,slhd->shbl", grad_pair, value_pair, preferred_element_type=jnp.float32
        )
        row_dot = jnp.sum(probs_exact * d_probs, axis=-1, keepdims=True)
        d_scores = (probs_exact * (d_probs - row_dot) * score_scale).astype(jnp.bfloat16)
        probs = probs_exact.astype(jnp.bfloat16)
        d_query = jnp.einsum(
            "shbl,slhd->sbhd", d_scores, key_pair, preferred_element_type=jnp.float32
        )
        d_key = jnp.einsum(
            "shbl,sbhd->slhd", d_scores, query_pair, preferred_element_type=jnp.float32
        )
        d_value = jnp.einsum(
            "shbl,sbhd->slhd", probs, grad_pair, preferred_element_type=jnp.float32
        )
        return (
            d_query.reshape(seqs_here, block, pair_width),
            d_key.reshape(seqs_here, full_len, pair_width),
            d_value.reshape(seqs_here, full_len, pair_width),
        )

    query_pairs, key_pairs, value_pairs = lax.map(backward_pair, (jnp.arange(pair_count), log_sums))
    key_pairs, value_pairs = (
        lax.psum_scatter(key_pairs, "seq", scatter_dimension=2, tiled=True),
        lax.psum_scatter(value_pairs, "seq", scatter_dimension=2, tiled=True),
    )
    d_query = heads_side(query_pairs)
    d_key = heads_side(key_pairs)
    d_value = heads_side(value_pairs)
    d_qkv = jnp.concatenate([d_query, d_key, d_value], axis=1).astype(jnp.bfloat16)
    qkv_weight_grad = jnp.dot(tokens.T, d_qkv, preferred_element_type=jnp.float32)
    query_bias_grad = jnp.sum(d_query, axis=0)
    value_bias_grad = jnp.sum(d_value, axis=0)
    grad_in = d_first + jnp.dot(d_qkv, w_qkv.T, preferred_element_type=jnp.float32)
    grads = (
        qkv_weight_grad,
        query_bias_grad,
        value_bias_grad,
        out_weight_grad,
        out_bias_grad,
        attn_gain_grad,
        attn_shift_grad,
        up_weight_grad,
        up_bias_grad,
        down_weight_grad,
        down_bias_grad,
        ffn_gain_grad,
        ffn_shift_grad,
    )
    owned = (
        lax.psum_scatter(grads[0], "dp", scatter_dimension=0, tiled=True),
        lax.psum_scatter(grads[1], "dp", scatter_dimension=0, tiled=True),
        lax.psum_scatter(grads[2], "dp", scatter_dimension=0, tiled=True),
        lax.psum_scatter(grads[3], "dp", scatter_dimension=0, tiled=True),
        lax.psum_scatter(grads[4], "dp", scatter_dimension=0, tiled=True),
        lax.psum_scatter(grads[5], "dp", scatter_dimension=0, tiled=True),
        lax.psum_scatter(grads[6], "dp", scatter_dimension=0, tiled=True),
        lax.psum_scatter(grads[7], "dp", scatter_dimension=0, tiled=True),
        lax.psum_scatter(grads[8], "dp", scatter_dimension=0, tiled=True),
        lax.psum_scatter(grads[9], "dp", scatter_dimension=0, tiled=True),
        lax.psum_scatter(grads[10], "dp", scatter_dimension=0, tiled=True),
        lax.psum_scatter(grads[11], "dp", scatter_dimension=0, tiled=True),
        lax.psum_scatter(grads[12], "dp", scatter_dimension=0, tiled=True),
    )
    owned = lax.psum(
        (
            owned[0],
            owned[1],
            owned[2],
            owned[3],
            owned[4],
            owned[5],
            owned[6],
            owned[7],
            owned[8],
            owned[9],
            owned[10],
            owned[11],
            owned[12],
        ),
        "seq",
    )
    return (layer_out.reshape(seqs_here, block, D), grad_in.reshape(seqs_here, block, D)) + tuple(
        owned
    )


def split_fits(mesh, heads, width, hidden):
    dp, seq = mesh.shape["dp"], mesh.shape["seq"]
    return heads % seq == 0 and width % (dp * seq) == 0 and hidden % (dp * seq) == 0


def gather_seq(array):
    return lax.all_gather(array, "seq", axis=1, tiled=True)


def scatter_seq(partial):
    seqs_here, full_len, width = partial.shape
    count = lax.axis_size("seq")
    pieces = partial.astype(jnp.bfloat16).reshape(seqs_here, count, full_len // count, width)
    got = lax.all_to_all(pieces, "seq", 1, 1)
    return jnp.sum(got.astype(jnp.float32), axis=1)


def scatter_dp(grads):
    return lax.psum_scatter(grads.astype(jnp.bfloat16), "dp", scatter_dimension=0, tiled=True)


def on_device(
    layer_in,
    lengths,
    qkv_weight,
    query_bias,
    value_bias,
    out_weight,
    out_bias,
    attn_gain,
    attn_shift,
    up_weight,
    up_bias,
    down_weight,
    down_bias,
    ffn_gain,
    ffn_shift,
    grad_out,
):
    f32, bf16 = jnp.float32, jnp.bfloat16
    parts, me = lax.axis_size("seq"), lax.axis_index("seq")
    owners = lax.axis_size("dp")
    seqs_here, block, width = layer_in.shape
    full_len = block * parts
    own = qkv_weight.shape[0]
    heads = H // parts
    cols = heads * HD
    hidden = up_weight.shape[1]
    unit = hidden // (owners * parts)
    hidden_part = owners * unit
    score_scale = HD ** (-0.5)

    def dot(a, b):
        return jnp.dot(a, b, preferred_element_type=f32)

    def flat(array):
        return array.reshape(-1, array.shape[-1])

    qkv_mine = lax.dynamic_index_in_dim(
        qkv_weight.reshape(own, 3, parts, cols), me, 2, keepdims=False
    ).reshape(own, 3 * cols)
    up_mine = lax.dynamic_index_in_dim(
        up_weight.reshape(own, owners, parts, unit), me, 2, keepdims=False
    ).reshape(own, hidden_part)
    down_mine = lax.dynamic_slice_in_dim(down_weight, me * unit, unit, 0)
    up_bias_mine = lax.dynamic_slice_in_dim(up_bias, me * unit, unit, 0)
    small = jnp.stack(
        [
            query_bias,
            value_bias,
            out_bias,
            attn_gain,
            attn_shift,
            down_bias,
            ffn_gain,
            ffn_shift,
            up_bias_mine,
        ],
        axis=1,
    )
    small = jnp.pad(small, ((0, 0), (0, 128 - small.shape[1])))
    tokens = gather_seq(layer_in)
    early = lax.all_gather(
        jnp.concatenate([out_weight, small, qkv_mine], axis=1), "dp", axis=0, tiled=True
    )
    late = lax.all_gather(
        jnp.concatenate([up_mine, down_mine], axis=1), "dp", axis=0, tiled=True
    )
    w_out = early[:, :width]
    vectors = early[:, width : width + 128].T.astype(f32)
    w_qkv = early[:, width + 128 :]
    w_up = late[:, :hidden_part]
    w_down = late[:, hidden_part:]
    q_bias, v_bias, b_out, gain_one, shift_one, b_down, gain_two, shift_two, b_up = [
        vectors[k] for k in range(9)
    ]

    def mine(vector):
        return lax.dynamic_slice_in_dim(vector, me * cols, cols, 0)

    bias_qkv = jnp.concatenate([mine(q_bias), jnp.zeros((cols,), f32), mine(v_bias)])
    tokens_flat = flat(tokens)
    qkv = (dot(tokens_flat, w_qkv) + bias_qkv).astype(bf16)
    qkv = qkv.reshape(seqs_here, full_len, 3, heads, HD).transpose(2, 0, 3, 1, 4)
    queries, keys, values = qkv[0], qkv[1], qkv[2]
    valid = jnp.arange(full_len)[None, :] < lengths[:, None]
    scores = jnp.einsum("shbd,shld->shbl", queries, keys, preferred_element_type=f32)
    scores = jnp.where(valid[:, None, None, :], scores * score_scale, mask_fill)
    row_top = jnp.max(scores, axis=-1, keepdims=True)
    log_sum = row_top + jnp.log(jnp.sum(jnp.exp(scores - row_top), axis=-1, keepdims=True))
    probs_exact = jnp.exp(scores - log_sum)
    probs = probs_exact.astype(bf16)
    mixed = jnp.einsum("shbl,shld->shbd", probs, values, preferred_element_type=f32)
    mixed = mixed.astype(bf16).transpose(0, 2, 1, 3).reshape(seqs_here, full_len, cols)
    attended = lax.all_gather(mixed, "seq", axis=2, tiled=True)
    attended_flat = flat(attended)
    first_sum = tokens_flat.astype(f32) + dot(attended_flat, w_out) + b_out
    first_norm, normed_all, inverse_all = layer_norm(first_sum, gain_one, shift_one)

    def here(rows):
        rows = rows.reshape(seqs_here, full_len, rows.shape[-1])
        return flat(lax.dynamic_slice_in_dim(rows, me * block, block, 1))

    normed_one, inverse_one = here(normed_all), here(inverse_all)
    first_round = first_norm.astype(bf16)
    inner = dot(first_round, w_up) + b_up
    activated = gelu_exact(inner).astype(bf16)
    down = flat(scatter_seq(dot(activated, w_down).reshape(seqs_here, full_len, width)))
    second_sum = here(first_norm) + down + b_down
    layer_out, normed_two, inverse_two = layer_norm(second_sum, gain_two, shift_two)

    upstream = flat(grad_out).astype(f32)
    ffn_gain_grad = jnp.sum(upstream * normed_two, axis=0)
    ffn_shift_grad = jnp.sum(upstream, axis=0)
    d_second = norm_back(upstream, normed_two, inverse_two, gain_two)
    d_second_all = flat(gather_seq(d_second.astype(bf16).reshape(seqs_here, block, width)))
    down_bias_grad = jnp.sum(d_second, axis=0)
    d_inner = dot(d_second_all, w_down.T) * gelu_slope(inner)
    d_inner_round = d_inner.astype(bf16)
    d_up = flat(scatter_seq(dot(d_inner_round, w_up.T).reshape(seqs_here, full_len, width)))
    down_weight_grad = dot(activated.T, d_second_all)
    up_weight_grad = dot(first_round.T, d_inner_round)
    up_bias_grad = jnp.sum(d_inner, axis=0)
    late_grads = scatter_dp(jnp.concatenate([up_weight_grad, down_weight_grad], axis=1))
    d_first_norm = d_second + d_up
    attn_gain_grad = jnp.sum(d_first_norm * normed_one, axis=0)
    attn_shift_grad = jnp.sum(d_first_norm, axis=0)
    d_first = norm_back(d_first_norm, normed_one, inverse_one, gain_one)
    out_bias_grad = jnp.sum(d_first, axis=0)
    d_first_all = flat(gather_seq(d_first.astype(bf16).reshape(seqs_here, block, width)))
    out_weight_grad = dot(
        attended_flat.T, lax.dynamic_slice_in_dim(d_first_all, me * cols, cols, 1)
    )
    w_out_mine = lax.dynamic_slice_in_dim(w_out, me * cols, cols, 0)
    d_attended = dot(d_first_all, w_out_mine.T).astype(bf16)
    d_attended = d_attended.reshape(seqs_here, full_len, heads, HD).transpose(0, 2, 1, 3)
    d_probs = jnp.einsum("shbd,shld->shbl", d_attended, values, preferred_element_type=f32)
    row_dot = jnp.sum(probs_exact * d_probs, axis=-1, keepdims=True)
    d_scores = (probs_exact * (d_probs - row_dot) * score_scale).astype(bf16)
    d_query = jnp.einsum("shbl,shld->shbd", d_scores, keys, preferred_element_type=f32)
    d_key = jnp.einsum("shbl,shbd->shld", d_scores, queries, preferred_element_type=f32)
    d_value = jnp.einsum("shbl,shbd->shld", probs, d_attended, preferred_element_type=f32)
    query_bias_grad = jnp.sum(d_query, axis=(0, 2)).reshape(cols)
    value_bias_grad = jnp.sum(d_value, axis=(0, 2)).reshape(cols)
    d_qkv = jnp.stack([d_query, d_key, d_value]).astype(bf16)
    d_qkv = d_qkv.transpose(1, 3, 0, 2, 4).reshape(seqs_here * full_len, 3 * cols)
    qkv_weight_grad = dot(tokens_flat.T, d_qkv)

    def placed(vector):
        return lax.dynamic_update_slice_in_dim(jnp.zeros((width,), f32), vector, me * cols, 0)

    small_grads = jnp.stack(
        [
            placed(query_bias_grad),
            placed(value_bias_grad),
            out_bias_grad,
            attn_gain_grad,
            attn_shift_grad,
            down_bias_grad,
            ffn_gain_grad,
            ffn_shift_grad,
            up_bias_grad,
        ]
    )
    small_grads = jnp.pad(small_grads, ((0, 128 - small_grads.shape[0]), (0, 0))).T
    early_grads = scatter_dp(
        jnp.concatenate([small_grads, qkv_weight_grad, out_weight_grad], axis=1)
    )
    d_in = flat(scatter_seq(dot(d_qkv, w_qkv.T).reshape(seqs_here, full_len, width)))
    grad_in = d_first + d_in

    late_all = lax.all_gather(late_grads, "seq", axis=0)
    early_all = lax.all_gather(early_grads, "seq", axis=0)
    up_owned = late_all[:, :, :hidden_part].reshape(parts, own, owners, unit)
    up_owned = up_owned.transpose(1, 2, 0, 3).reshape(own, hidden).astype(f32)
    down_owned = late_all[:, :, hidden_part:].reshape(parts * unit, width).astype(f32)
    small_owned = early_all[:, :, :128].astype(f32)
    sums = jnp.sum(small_owned, axis=0).T
    up_bias_owned = small_owned[:, :, 8].reshape(parts * unit)
    qkv_owned = early_all[:, :, 128 : 128 + 3 * cols].reshape(parts, own, 3, cols)
    qkv_owned = qkv_owned.transpose(1, 2, 0, 3).reshape(own, 3 * width).astype(f32)
    out_owned = early_all[:, :, 128 + 3 * cols :].transpose(1, 0, 2).reshape(own, width)
    return (
        layer_out.reshape(seqs_here, block, width),
        grad_in.reshape(seqs_here, block, width),
        qkv_owned,
        sums[0],
        sums[1],
        out_owned.astype(f32),
        sums[2],
        sums[3],
        sums[4],
        up_owned,
        up_bias_owned,
        down_owned,
        sums[5],
        sums[6],
        sums[7],
    )


def solution(mesh):
    in_specs = (
        P("dp", "seq", None),
        P("dp"),
        P("dp", None),
        P("dp"),
        P("dp"),
        P("dp", None),
        P("dp"),
        P("dp"),
        P("dp"),
        P("dp", None),
        P("dp"),
        P("dp", None),
        P("dp"),
        P("dp"),
        P("dp"),
        P("dp", "seq", None),
    )
    out_specs = (
        P("dp", "seq", None),
        P("dp", "seq", None),
        P("dp", None),
        P("dp"),
        P("dp"),
        P("dp", None),
        P("dp"),
        P("dp"),
        P("dp"),
        P("dp", None),
        P("dp"),
        P("dp", None),
        P("dp"),
        P("dp"),
        P("dp"),
    )
    body = on_device if split_fits(mesh, H, D, FF) else on_device_general
    return jax.shard_map(
        body, mesh=mesh, in_specs=in_specs, out_specs=out_specs, check_vma=False
    )
```

```python
import functools
import math

import jax
import jax.numpy as jnp
from jax import lax
from jax.experimental import pallas as pl
from jax.experimental.pallas import tpu as pltpu
from jax.sharding import PartitionSpec as P

D = 768
H = 12
HD = 64
FF = 3072


norm_eps = 1e-12
mask_fill = -1e30


def layer_norm(hidden, gain, shift):
    centred = hidden - jnp.mean(hidden, axis=-1, keepdims=True)
    inverse = lax.rsqrt(jnp.mean(centred * centred, axis=-1, keepdims=True) + norm_eps)
    normed = centred * inverse
    return (normed * gain + shift, normed, inverse)


def norm_back(grad_norm, normed, inverse, gain):
    scaled = grad_norm * gain
    middle = scaled - jnp.mean(scaled, axis=-1, keepdims=True)
    return inverse * (middle - normed * jnp.mean(scaled * normed, axis=-1, keepdims=True))


def gelu_exact(inner):
    return 0.5 * inner * (1.0 + jax.scipy.special.erf(inner * (1.0 / math.sqrt(2.0))))


def gelu_slope(inner):
    cumul = 0.5 * (1.0 + jax.scipy.special.erf(inner * (1.0 / math.sqrt(2.0))))
    return cumul + inner * jnp.exp(-0.5 * inner * inner) * (1.0 / math.sqrt(2.0 * math.pi))


def on_device_general(
    layer_in,
    lengths,
    qkv_weight,
    query_bias,
    value_bias,
    out_weight,
    out_bias,
    attn_gain,
    attn_shift,
    up_weight,
    up_bias,
    down_weight,
    down_bias,
    ffn_gain,
    ffn_shift,
    grad_out,
):
    params = (
        qkv_weight,
        query_bias,
        value_bias,
        out_weight,
        out_bias,
        attn_gain,
        attn_shift,
        up_weight,
        up_bias,
        down_weight,
        down_bias,
        ffn_gain,
        ffn_shift,
    )
    gathered = (
        lax.all_gather(params[0], "dp", axis=0, tiled=True),
        lax.all_gather(params[1], "dp", axis=0, tiled=True),
        lax.all_gather(params[2], "dp", axis=0, tiled=True),
        lax.all_gather(params[3], "dp", axis=0, tiled=True),
        lax.all_gather(params[4], "dp", axis=0, tiled=True),
        lax.all_gather(params[5], "dp", axis=0, tiled=True),
        lax.all_gather(params[6], "dp", axis=0, tiled=True),
        lax.all_gather(params[7], "dp", axis=0, tiled=True),
        lax.all_gather(params[8], "dp", axis=0, tiled=True),
        lax.all_gather(params[9], "dp", axis=0, tiled=True),
        lax.all_gather(params[10], "dp", axis=0, tiled=True),
        lax.all_gather(params[11], "dp", axis=0, tiled=True),
        lax.all_gather(params[12], "dp", axis=0, tiled=True),
    )
    (
        w_qkv,
        q_bias,
        v_bias,
        w_out,
        b_out,
        gain_raw,
        shift_raw,
        w_up,
        b_up,
        w_down,
        b_down,
        gain_last,
        shift_last,
    ) = gathered
    seqs_here, block, width_model = layer_in.shape
    full_len = block * lax.axis_size("seq")
    rows = seqs_here * block
    pair_width = 2 * HD
    pair_count = H // 2
    score_scale = HD ** (-0.5)
    bias_qkv = jnp.concatenate(
        [q_bias.astype(jnp.float32), jnp.zeros((D,), jnp.float32), v_bias.astype(jnp.float32)]
    )
    gain_one = gain_raw.astype(jnp.float32)
    shift_one = shift_raw.astype(jnp.float32)
    gain_two = gain_last.astype(jnp.float32)
    shift_two = shift_last.astype(jnp.float32)
    tokens = layer_in.reshape(rows, D)
    qkv_proj = (jnp.dot(tokens, w_qkv, preferred_element_type=jnp.float32) + bias_qkv).astype(
        jnp.bfloat16
    )
    qkv_proj = qkv_proj.reshape(seqs_here, block, 3 * D)
    queries = qkv_proj[:, :, :D]
    keys_here = qkv_proj[:, :, D : 2 * D]
    values_here = qkv_proj[:, :, 2 * D :]
    keys_all, values_all = (
        lax.all_gather(keys_here, "seq", axis=1, tiled=True),
        lax.all_gather(values_here, "seq", axis=1, tiled=True),
    )
    valid = jnp.arange(full_len)[None, :] < lengths[:, None]

    def pair_part(array, pair_idx):
        piece = lax.dynamic_slice_in_dim(array, pair_idx * pair_width, pair_width, 2)
        return piece.reshape(piece.shape[:2] + (2, HD))

    def pair_scores(query_pair, key_pair):
        scores = (
            jnp.einsum("sbhd,slhd->shbl", query_pair, key_pair, preferred_element_type=jnp.float32)
            * score_scale
        )
        return jnp.where(valid[:, None, None, :], scores, mask_fill)

    def forward_pair(pair_idx):
        query_pair = pair_part(queries, pair_idx)
        key_pair = pair_part(keys_all, pair_idx)
        value_pair = pair_part(values_all, pair_idx)
        scores = pair_scores(query_pair, key_pair)
        row_top = jnp.max(scores, axis=-1, keepdims=True)
        log_sum = row_top + jnp.log(jnp.sum(jnp.exp(scores - row_top), axis=-1, keepdims=True))
        probs = jnp.exp(scores - log_sum).astype(jnp.bfloat16)
        mixed = jnp.einsum("shbl,slhd->sbhd", probs, value_pair, preferred_element_type=jnp.float32)
        return (mixed.astype(jnp.bfloat16).reshape(seqs_here, block, pair_width), log_sum)

    pair_out, log_sums = lax.map(forward_pair, jnp.arange(pair_count))

    def heads_side(stacked):
        return jnp.transpose(stacked, (1, 2, 0, 3)).reshape(rows, D)

    attended = heads_side(pair_out)
    first_sum = (
        tokens.astype(jnp.float32)
        + jnp.dot(attended, w_out, preferred_element_type=jnp.float32)
        + b_out.astype(jnp.float32)
    )
    first_norm, normed_one, inverse_one = layer_norm(first_sum, gain_one, shift_one)
    first_round = first_norm.astype(jnp.bfloat16)
    inner = jnp.dot(first_round, w_up, preferred_element_type=jnp.float32) + b_up.astype(
        jnp.float32
    )
    activated = gelu_exact(inner).astype(jnp.bfloat16)
    second_sum = (
        first_norm
        + jnp.dot(activated, w_down, preferred_element_type=jnp.float32)
        + b_down.astype(jnp.float32)
    )
    layer_out, normed_two, inverse_two = layer_norm(second_sum, gain_two, shift_two)
    (
        w_qkv,
        q_bias,
        v_bias,
        w_out,
        b_out,
        gain_raw,
        shift_raw,
        w_up,
        b_up,
        w_down,
        b_down,
        gain_last,
        shift_last,
    ) = (
        lax.all_gather(params[0], "dp", axis=0, tiled=True),
        lax.all_gather(params[1], "dp", axis=0, tiled=True),
        lax.all_gather(params[2], "dp", axis=0, tiled=True),
        lax.all_gather(params[3], "dp", axis=0, tiled=True),
        lax.all_gather(params[4], "dp", axis=0, tiled=True),
        lax.all_gather(params[5], "dp", axis=0, tiled=True),
        lax.all_gather(params[6], "dp", axis=0, tiled=True),
        lax.all_gather(params[7], "dp", axis=0, tiled=True),
        lax.all_gather(params[8], "dp", axis=0, tiled=True),
        lax.all_gather(params[9], "dp", axis=0, tiled=True),
        lax.all_gather(params[10], "dp", axis=0, tiled=True),
        lax.all_gather(params[11], "dp", axis=0, tiled=True),
        lax.all_gather(params[12], "dp", axis=0, tiled=True),
    )
    gain_one = gain_raw.astype(jnp.float32)
    gain_two = gain_last.astype(jnp.float32)
    upstream = grad_out.reshape(rows, D).astype(jnp.float32)
    ffn_gain_grad = jnp.sum(upstream * normed_two, axis=0)
    ffn_shift_grad = jnp.sum(upstream, axis=0)
    d_second = norm_back(upstream, normed_two, inverse_two, gain_two)
    d_second_round = d_second.astype(jnp.bfloat16)
    down_weight_grad = jnp.dot(activated.T, d_second_round, preferred_element_type=jnp.float32)
    down_bias_grad = jnp.sum(d_second, axis=0)
    d_inner = jnp.dot(d_second_round, w_down.T, preferred_element_type=jnp.float32) * gelu_slope(
        inner
    )
    d_inner_round = d_inner.astype(jnp.bfloat16)
    up_weight_grad = jnp.dot(first_round.T, d_inner_round, preferred_element_type=jnp.float32)
    up_bias_grad = jnp.sum(d_inner, axis=0)
    d_first_norm = d_second + jnp.dot(d_inner_round, w_up.T, preferred_element_type=jnp.float32)
    attn_gain_grad = jnp.sum(d_first_norm * normed_one, axis=0)
    attn_shift_grad = jnp.sum(d_first_norm, axis=0)
    d_first = norm_back(d_first_norm, normed_one, inverse_one, gain_one)
    d_first_round = d_first.astype(jnp.bfloat16)
    out_weight_grad = jnp.dot(attended.T, d_first_round, preferred_element_type=jnp.float32)
    out_bias_grad = jnp.sum(d_first, axis=0)
    d_attended = jnp.dot(d_first_round, w_out.T, preferred_element_type=jnp.float32).astype(
        jnp.bfloat16
    )
    d_attended = d_attended.reshape(seqs_here, block, D)

    def backward_pair(item):
        pair_idx, log_sum = item
        query_pair = pair_part(queries, pair_idx)
        key_pair = pair_part(keys_all, pair_idx)
        value_pair = pair_part(values_all, pair_idx)
        grad_pair = pair_part(d_attended, pair_idx)
        probs_exact = jnp.exp(pair_scores(query_pair, key_pair) - log_sum)
        d_probs = jnp.einsum(
            "sbhd,slhd->shbl", grad_pair, value_pair, preferred_element_type=jnp.float32
        )
        row_dot = jnp.sum(probs_exact * d_probs, axis=-1, keepdims=True)
        d_scores = (probs_exact * (d_probs - row_dot) * score_scale).astype(jnp.bfloat16)
        probs = probs_exact.astype(jnp.bfloat16)
        d_query = jnp.einsum(
            "shbl,slhd->sbhd", d_scores, key_pair, preferred_element_type=jnp.float32
        )
        d_key = jnp.einsum(
            "shbl,sbhd->slhd", d_scores, query_pair, preferred_element_type=jnp.float32
        )
        d_value = jnp.einsum(
            "shbl,sbhd->slhd", probs, grad_pair, preferred_element_type=jnp.float32
        )
        return (
            d_query.reshape(seqs_here, block, pair_width),
            d_key.reshape(seqs_here, full_len, pair_width),
            d_value.reshape(seqs_here, full_len, pair_width),
        )

    query_pairs, key_pairs, value_pairs = lax.map(backward_pair, (jnp.arange(pair_count), log_sums))
    key_pairs, value_pairs = (
        lax.psum_scatter(key_pairs, "seq", scatter_dimension=2, tiled=True),
        lax.psum_scatter(value_pairs, "seq", scatter_dimension=2, tiled=True),
    )
    d_query = heads_side(query_pairs)
    d_key = heads_side(key_pairs)
    d_value = heads_side(value_pairs)
    d_qkv = jnp.concatenate([d_query, d_key, d_value], axis=1).astype(jnp.bfloat16)
    qkv_weight_grad = jnp.dot(tokens.T, d_qkv, preferred_element_type=jnp.float32)
    query_bias_grad = jnp.sum(d_query, axis=0)
    value_bias_grad = jnp.sum(d_value, axis=0)
    grad_in = d_first + jnp.dot(d_qkv, w_qkv.T, preferred_element_type=jnp.float32)
    grads = (
        qkv_weight_grad,
        query_bias_grad,
        value_bias_grad,
        out_weight_grad,
        out_bias_grad,
        attn_gain_grad,
        attn_shift_grad,
        up_weight_grad,
        up_bias_grad,
        down_weight_grad,
        down_bias_grad,
        ffn_gain_grad,
        ffn_shift_grad,
    )
    owned = (
        lax.psum_scatter(grads[0], "dp", scatter_dimension=0, tiled=True),
        lax.psum_scatter(grads[1], "dp", scatter_dimension=0, tiled=True),
        lax.psum_scatter(grads[2], "dp", scatter_dimension=0, tiled=True),
        lax.psum_scatter(grads[3], "dp", scatter_dimension=0, tiled=True),
        lax.psum_scatter(grads[4], "dp", scatter_dimension=0, tiled=True),
        lax.psum_scatter(grads[5], "dp", scatter_dimension=0, tiled=True),
        lax.psum_scatter(grads[6], "dp", scatter_dimension=0, tiled=True),
        lax.psum_scatter(grads[7], "dp", scatter_dimension=0, tiled=True),
        lax.psum_scatter(grads[8], "dp", scatter_dimension=0, tiled=True),
        lax.psum_scatter(grads[9], "dp", scatter_dimension=0, tiled=True),
        lax.psum_scatter(grads[10], "dp", scatter_dimension=0, tiled=True),
        lax.psum_scatter(grads[11], "dp", scatter_dimension=0, tiled=True),
        lax.psum_scatter(grads[12], "dp", scatter_dimension=0, tiled=True),
    )
    owned = lax.psum(
        (
            owned[0],
            owned[1],
            owned[2],
            owned[3],
            owned[4],
            owned[5],
            owned[6],
            owned[7],
            owned[8],
            owned[9],
            owned[10],
            owned[11],
            owned[12],
        ),
        "seq",
    )
    return (layer_out.reshape(seqs_here, block, D), grad_in.reshape(seqs_here, block, D)) + tuple(
        owned
    )


def split_fits(mesh, heads, width, hidden):
    dp, seq = mesh.shape["dp"], mesh.shape["seq"]
    return heads % seq == 0 and dp % 2 == 0 and width % (dp * seq) == 0 and hidden % (dp * seq) == 0


def remote(src, dst, send_sem, recv_sem, peer):
    copy = pltpu.make_async_remote_copy(
        src_ref=src,
        dst_ref=dst,
        send_sem=send_sem,
        recv_sem=recv_sem,
        device_id=peer,
        device_id_type=pl.DeviceIdType.MESH,
    )
    copy.start()
    return copy


def greet(peers):
    barrier = pltpu.get_barrier_semaphore()
    for peer in peers:
        pl.semaphore_signal(
            barrier, inc=1, device_id=peer, device_id_type=pl.DeviceIdType.MESH
        )
    pl.semaphore_wait(barrier, len(peers))


def places(owners, parts):
    at = lax.axis_index("dp")
    line, side = at // 2, at % 2
    lines = owners // 2
    me = lax.axis_index("seq")
    line_peers = [{"dp": ((line + k) % lines) * 2 + side} for k in range(1, lines)]
    seq_peers = [{"seq": (me + k) % parts} for k in range(1, parts)]
    return line, side, lines, me, line_peers, {"dp": line * 2 + 1 - side}, seq_peers


def start_kernel(
    owners, parts, x_ref, w_ref, x_out, w_out, x_send, x_recv, l_send, l_recv, p_send, p_recv
):
    line, side, lines, me, line_peers, pair, seq_peers = places(owners, parts)
    greet(line_peers + [pair] + seq_peers)
    block = x_ref.shape[1]
    mine = line * 2 + side
    rows = pl.ds(pl.multiple_of(me * block, block), block)
    copies = []
    for k, peer in enumerate(line_peers):
        copies.append(remote(w_ref, w_out.at[mine], l_send.at[k], l_recv.at[k], peer))
    paired = [remote(w_ref, w_out.at[mine], p_send.at[0], p_recv.at[0], pair)]
    tokens = []
    for k, peer in enumerate(seq_peers):
        tokens.append(remote(x_ref, x_out.at[:, rows, :], x_send.at[k], x_recv.at[k], peer))
    w_out[mine] = w_ref[...]
    x_out[:, rows, :] = x_ref[...]
    for k in range(1, lines):
        copies[k - 1].wait_recv()
        slot = w_out.at[((line + lines - k) % lines) * 2 + side]
        paired.append(remote(slot, slot, p_send.at[k], p_recv.at[k], pair))
    for copy in copies:
        copy.wait_send()
    for copy in paired + tokens:
        copy.wait()


def gather_start(layer_in, weights, owners, parts):
    seqs_here, block, width = layer_in.shape
    own, cols = weights.shape
    vmem = pl.BlockSpec(memory_space=pltpu.VMEM)
    dma = pltpu.SemaphoreType.DMA
    lines = owners // 2
    return pl.pallas_call(
        functools.partial(start_kernel, owners, parts),
        out_shape=(
            jax.ShapeDtypeStruct((seqs_here, block * parts, width), layer_in.dtype),
            jax.ShapeDtypeStruct((owners, own, cols), weights.dtype),
        ),
        in_specs=[vmem, vmem],
        out_specs=(vmem, vmem),
        scratch_shapes=[
            dma((parts - 1,)),
            dma((parts - 1,)),
            dma((lines - 1,)),
            dma((lines - 1,)),
            dma((lines,)),
            dma((lines,)),
        ],
        compiler_params=pltpu.CompilerParams(collective_id=0, has_side_effects=True),
        cost_estimate=pl.CostEstimate(flops=0, bytes_accessed=80_000_000, transcendentals=0),
    )(layer_in, weights)


def end_kernel(
    owners,
    parts,
    g_ref,
    d_ref,
    g_out,
    d_out,
    pair_in,
    line_out,
    line_in,
    total,
    d_send,
    d_recv,
    p_send,
    p_recv,
    l_send,
    l_recv,
    s_send,
    s_recv,
):
    line, side, lines, me, line_peers, pair, seq_peers = places(owners, parts)
    greet(line_peers + [pair] + seq_peers)
    block = d_ref.shape[1] // parts
    order = list(range(1, lines)) + [0]
    paired = {}
    for k in order:
        owner = ((line + k) % lines) * 2
        paired[k] = remote(
            g_ref.at[owner + 1 - side], pair_in.at[k], p_send.at[k], p_recv.at[k], pair
        )
    inputs = []
    for k, peer in enumerate(seq_peers):
        start = pl.multiple_of(((me + k + 1) % parts) * block, block)
        piece = d_ref.at[:, pl.ds(start, block), :]
        inputs.append(remote(piece, d_out.at[k], d_send.at[k], d_recv.at[k], peer))
    lined = []
    for k in range(1, lines):
        paired[k].wait_recv()
        owner = ((line + k) % lines) * 2
        both = g_ref[owner + side].astype(jnp.float32) + pair_in[k].astype(jnp.float32)
        line_out[k - 1] = both.astype(line_out.dtype)
        lined.append(
            remote(
                line_out.at[k - 1],
                line_in.at[k - 1],
                l_send.at[k - 1],
                l_recv.at[k - 1],
                line_peers[k - 1],
            )
        )
    paired[0].wait_recv()
    held = g_ref[line * 2 + side].astype(jnp.float32) + pair_in[0].astype(jnp.float32)
    for k in range(1, lines):
        lined[k - 1].wait_recv()
        held = held + line_in[k - 1].astype(jnp.float32)
    total[...] = held.astype(total.dtype)
    g_out[me] = held.astype(g_out.dtype)
    shared = []
    for k, peer in enumerate(seq_peers):
        shared.append(remote(total, g_out.at[me], s_send.at[k], s_recv.at[k], peer))
    for k in range(lines):
        paired[k].wait_send()
    for copy in lined:
        copy.wait_send()
    for copy in inputs + shared:
        copy.wait()


def scatter_end(grads, partial, owners, parts):
    rows, cols = grads.shape
    own, lines = rows // owners, owners // 2
    seqs_here, full_len, width = partial.shape
    block = full_len // parts
    vmem = pl.BlockSpec(memory_space=pltpu.VMEM)
    dma = pltpu.SemaphoreType.DMA
    dtype = grads.dtype
    return pl.pallas_call(
        functools.partial(end_kernel, owners, parts),
        out_shape=(
            jax.ShapeDtypeStruct((parts, own, cols), dtype),
            jax.ShapeDtypeStruct((parts - 1, seqs_here, block, width), partial.dtype),
        ),
        in_specs=[vmem, vmem],
        out_specs=(vmem, vmem),
        scratch_shapes=[
            pltpu.VMEM((lines, own, cols), dtype),
            pltpu.VMEM((lines - 1, own, cols), dtype),
            pltpu.VMEM((lines - 1, own, cols), dtype),
            pltpu.VMEM((own, cols), dtype),
            dma((parts - 1,)),
            dma((parts - 1,)),
            dma((lines,)),
            dma((lines,)),
            dma((lines - 1,)),
            dma((lines - 1,)),
            dma((parts - 1,)),
            dma((parts - 1,)),
        ],
        compiler_params=pltpu.CompilerParams(collective_id=1, has_side_effects=True),
        cost_estimate=pl.CostEstimate(flops=0, bytes_accessed=80_000_000, transcendentals=0),
    )(grads.reshape(owners, own, cols), partial)


def gather_seq(array):
    return lax.all_gather(array, "seq", axis=1, tiled=True)


def scatter_seq(partial):
    seqs_here, full_len, width = partial.shape
    count = lax.axis_size("seq")
    pieces = partial.astype(jnp.bfloat16).reshape(seqs_here, count, full_len // count, width)
    got = lax.all_to_all(pieces, "seq", 1, 1)
    return jnp.sum(got.astype(jnp.float32), axis=1)


def scatter_dp(grads):
    return lax.psum_scatter(grads.astype(jnp.bfloat16), "dp", scatter_dimension=0, tiled=True)


def on_device(
    layer_in,
    lengths,
    qkv_weight,
    query_bias,
    value_bias,
    out_weight,
    out_bias,
    attn_gain,
    attn_shift,
    up_weight,
    up_bias,
    down_weight,
    down_bias,
    ffn_gain,
    ffn_shift,
    grad_out,
):
    f32, bf16 = jnp.float32, jnp.bfloat16
    parts, me = lax.axis_size("seq"), lax.axis_index("seq")
    owners = lax.axis_size("dp")
    seqs_here, block, width = layer_in.shape
    full_len = block * parts
    own = qkv_weight.shape[0]
    heads = H // parts
    cols = heads * HD
    hidden = up_weight.shape[1]
    unit = hidden // (owners * parts)
    hidden_part = owners * unit
    score_scale = HD ** (-0.5)

    def dot(a, b):
        return jnp.dot(a, b, preferred_element_type=f32)

    def flat(array):
        return array.reshape(-1, array.shape[-1])

    qkv_mine = lax.dynamic_index_in_dim(
        qkv_weight.reshape(own, 3, parts, cols), me, 2, keepdims=False
    ).reshape(own, 3 * cols)
    up_mine = lax.dynamic_index_in_dim(
        up_weight.reshape(own, owners, parts, unit), me, 2, keepdims=False
    ).reshape(own, hidden_part)
    down_mine = lax.dynamic_slice_in_dim(down_weight, me * unit, unit, 0)
    up_bias_mine = lax.dynamic_slice_in_dim(up_bias, me * unit, unit, 0)
    small = jnp.stack(
        [
            query_bias,
            value_bias,
            out_bias,
            attn_gain,
            attn_shift,
            down_bias,
            ffn_gain,
            ffn_shift,
            up_bias_mine,
        ],
        axis=1,
    )
    small = jnp.pad(small, ((0, 0), (0, 128 - small.shape[1])))
    tokens, early = gather_start(
        layer_in, jnp.concatenate([out_weight, small, qkv_mine], axis=1), owners, parts
    )
    early = flat(early)
    late = lax.all_gather(
        jnp.concatenate([up_mine, down_mine], axis=1), "dp", axis=0, tiled=True
    )
    w_out = early[:, :width]
    vectors = early[:, width : width + 128].T.astype(f32)
    w_qkv = early[:, width + 128 :]
    w_up = late[:, :hidden_part]
    w_down = late[:, hidden_part:]
    q_bias, v_bias, b_out, gain_one, shift_one, b_down, gain_two, shift_two, b_up = [
        vectors[k] for k in range(9)
    ]

    def mine(vector):
        return lax.dynamic_slice_in_dim(vector, me * cols, cols, 0)

    bias_qkv = jnp.concatenate([mine(q_bias), jnp.zeros((cols,), f32), mine(v_bias)])
    tokens_flat = flat(tokens)
    qkv = (dot(tokens_flat, w_qkv) + bias_qkv).astype(bf16)
    qkv = qkv.reshape(seqs_here, full_len, 3, heads, HD).transpose(2, 0, 3, 1, 4)
    queries, keys, values = qkv[0], qkv[1], qkv[2]
    valid = jnp.arange(full_len)[None, :] < lengths[:, None]
    scores = jnp.einsum("shbd,shld->shbl", queries, keys, preferred_element_type=f32)
    scores = jnp.where(valid[:, None, None, :], scores * score_scale, mask_fill)
    row_top = jnp.max(scores, axis=-1, keepdims=True)
    log_sum = row_top + jnp.log(jnp.sum(jnp.exp(scores - row_top), axis=-1, keepdims=True))
    probs_exact = jnp.exp(scores - log_sum)
    probs = probs_exact.astype(bf16)
    mixed = jnp.einsum("shbl,shld->shbd", probs, values, preferred_element_type=f32)
    mixed = mixed.astype(bf16).transpose(0, 2, 1, 3).reshape(seqs_here, full_len, cols)
    attended = lax.all_gather(mixed, "seq", axis=2, tiled=True)
    attended_flat = flat(attended)
    first_sum = tokens_flat.astype(f32) + dot(attended_flat, w_out) + b_out
    first_norm, normed_all, inverse_all = layer_norm(first_sum, gain_one, shift_one)

    def here(rows):
        rows = rows.reshape(seqs_here, full_len, rows.shape[-1])
        return flat(lax.dynamic_slice_in_dim(rows, me * block, block, 1))

    normed_one, inverse_one = here(normed_all), here(inverse_all)
    first_round = first_norm.astype(bf16)
    inner = dot(first_round, w_up) + b_up
    activated = gelu_exact(inner).astype(bf16)
    down = flat(scatter_seq(dot(activated, w_down).reshape(seqs_here, full_len, width)))
    second_sum = here(first_norm) + down + b_down
    layer_out, normed_two, inverse_two = layer_norm(second_sum, gain_two, shift_two)

    upstream = flat(grad_out).astype(f32)
    ffn_gain_grad = jnp.sum(upstream * normed_two, axis=0)
    ffn_shift_grad = jnp.sum(upstream, axis=0)
    d_second = norm_back(upstream, normed_two, inverse_two, gain_two)
    d_second_all = flat(gather_seq(d_second.astype(bf16).reshape(seqs_here, block, width)))
    down_bias_grad = jnp.sum(d_second, axis=0)
    d_inner = dot(d_second_all, w_down.T) * gelu_slope(inner)
    d_inner_round = d_inner.astype(bf16)
    d_up = flat(scatter_seq(dot(d_inner_round, w_up.T).reshape(seqs_here, full_len, width)))
    down_weight_grad = dot(activated.T, d_second_all)
    up_weight_grad = dot(first_round.T, d_inner_round)
    up_bias_grad = jnp.sum(d_inner, axis=0)
    late_grads = scatter_dp(jnp.concatenate([up_weight_grad, down_weight_grad], axis=1))
    d_first_norm = d_second + d_up
    attn_gain_grad = jnp.sum(d_first_norm * normed_one, axis=0)
    attn_shift_grad = jnp.sum(d_first_norm, axis=0)
    d_first = norm_back(d_first_norm, normed_one, inverse_one, gain_one)
    out_bias_grad = jnp.sum(d_first, axis=0)
    d_first_all = flat(gather_seq(d_first.astype(bf16).reshape(seqs_here, block, width)))
    out_weight_grad = dot(
        attended_flat.T, lax.dynamic_slice_in_dim(d_first_all, me * cols, cols, 1)
    )
    w_out_mine = lax.dynamic_slice_in_dim(w_out, me * cols, cols, 0)
    d_attended = dot(d_first_all, w_out_mine.T).astype(bf16)
    d_attended = d_attended.reshape(seqs_here, full_len, heads, HD).transpose(0, 2, 1, 3)
    d_probs = jnp.einsum("shbd,shld->shbl", d_attended, values, preferred_element_type=f32)
    row_dot = jnp.sum(probs_exact * d_probs, axis=-1, keepdims=True)
    d_scores = (probs_exact * (d_probs - row_dot) * score_scale).astype(bf16)
    d_query = jnp.einsum("shbl,shld->shbd", d_scores, keys, preferred_element_type=f32)
    d_key = jnp.einsum("shbl,shbd->shld", d_scores, queries, preferred_element_type=f32)
    d_value = jnp.einsum("shbl,shbd->shld", probs, d_attended, preferred_element_type=f32)
    query_bias_grad = jnp.sum(d_query, axis=(0, 2)).reshape(cols)
    value_bias_grad = jnp.sum(d_value, axis=(0, 2)).reshape(cols)
    d_qkv = jnp.stack([d_query, d_key, d_value]).astype(bf16)
    d_qkv = d_qkv.transpose(1, 3, 0, 2, 4).reshape(seqs_here * full_len, 3 * cols)
    qkv_weight_grad = dot(tokens_flat.T, d_qkv)

    def placed(vector):
        return lax.dynamic_update_slice_in_dim(jnp.zeros((width,), f32), vector, me * cols, 0)

    small_grads = jnp.stack(
        [
            placed(query_bias_grad),
            placed(value_bias_grad),
            out_bias_grad,
            attn_gain_grad,
            attn_shift_grad,
            down_bias_grad,
            ffn_gain_grad,
            ffn_shift_grad,
            up_bias_grad,
        ]
    )
    small_grads = jnp.pad(small_grads, ((0, 128 - small_grads.shape[0]), (0, 0))).T
    d_in = dot(d_qkv, w_qkv.T)
    early_all, d_others = scatter_end(
        jnp.concatenate([small_grads, qkv_weight_grad, out_weight_grad], axis=1).astype(bf16),
        d_in.reshape(seqs_here, full_len, width).astype(bf16),
        owners,
        parts,
    )
    grad_in = d_first + here(d_in) + flat(jnp.sum(d_others.astype(f32), axis=0))

    late_all = lax.all_gather(late_grads, "seq", axis=0)
    up_owned = late_all[:, :, :hidden_part].reshape(parts, own, owners, unit)
    up_owned = up_owned.transpose(1, 2, 0, 3).reshape(own, hidden).astype(f32)
    down_owned = late_all[:, :, hidden_part:].reshape(parts * unit, width).astype(f32)
    small_owned = early_all[:, :, :128].astype(f32)
    sums = jnp.sum(small_owned, axis=0).T
    up_bias_owned = small_owned[:, :, 8].reshape(parts * unit)
    qkv_owned = early_all[:, :, 128 : 128 + 3 * cols].reshape(parts, own, 3, cols)
    qkv_owned = qkv_owned.transpose(1, 2, 0, 3).reshape(own, 3 * width).astype(f32)
    out_owned = early_all[:, :, 128 + 3 * cols :].transpose(1, 0, 2).reshape(own, width)
    return (
        layer_out.reshape(seqs_here, block, width),
        grad_in.reshape(seqs_here, block, width),
        qkv_owned,
        sums[0],
        sums[1],
        out_owned.astype(f32),
        sums[2],
        sums[3],
        sums[4],
        up_owned,
        up_bias_owned,
        down_owned,
        sums[5],
        sums[6],
        sums[7],
    )


def solution(mesh):
    in_specs = (
        P("dp", "seq", None),
        P("dp"),
        P("dp", None),
        P("dp"),
        P("dp"),
        P("dp", None),
        P("dp"),
        P("dp"),
        P("dp"),
        P("dp", None),
        P("dp"),
        P("dp", None),
        P("dp"),
        P("dp"),
        P("dp"),
        P("dp", "seq", None),
    )
    out_specs = (
        P("dp", "seq", None),
        P("dp", "seq", None),
        P("dp", None),
        P("dp"),
        P("dp"),
        P("dp", None),
        P("dp"),
        P("dp"),
        P("dp"),
        P("dp", None),
        P("dp"),
        P("dp", None),
        P("dp"),
        P("dp"),
        P("dp"),
    )
    body = on_device if split_fits(mesh, H, D, FF) else on_device_general
    return jax.shard_map(
        body, mesh=mesh, in_specs=in_specs, out_specs=out_specs, check_vma=False
    )
```

```python
import functools
import math

import jax
import jax.numpy as jnp
from jax import lax
from jax.experimental import pallas as pl
from jax.experimental.pallas import tpu as pltpu
from jax.sharding import PartitionSpec as P

D = 768
H = 12
HD = 64
FF = 3072


norm_eps = 1e-12
mask_fill = -1e30


def layer_norm(hidden, gain, shift):
    centred = hidden - jnp.mean(hidden, axis=-1, keepdims=True)
    inverse = lax.rsqrt(jnp.mean(centred * centred, axis=-1, keepdims=True) + norm_eps)
    normed = centred * inverse
    return (normed * gain + shift, normed, inverse)


def norm_back(grad_norm, normed, inverse, gain):
    scaled = grad_norm * gain
    middle = scaled - jnp.mean(scaled, axis=-1, keepdims=True)
    return inverse * (middle - normed * jnp.mean(scaled * normed, axis=-1, keepdims=True))


def gelu_exact(inner):
    return 0.5 * inner * (1.0 + jax.scipy.special.erf(inner * (1.0 / math.sqrt(2.0))))


def gelu_slope(inner):
    cumul = 0.5 * (1.0 + jax.scipy.special.erf(inner * (1.0 / math.sqrt(2.0))))
    return cumul + inner * jnp.exp(-0.5 * inner * inner) * (1.0 / math.sqrt(2.0 * math.pi))


def on_device_general(
    layer_in,
    lengths,
    qkv_weight,
    query_bias,
    value_bias,
    out_weight,
    out_bias,
    attn_gain,
    attn_shift,
    up_weight,
    up_bias,
    down_weight,
    down_bias,
    ffn_gain,
    ffn_shift,
    grad_out,
):
    params = (
        qkv_weight,
        query_bias,
        value_bias,
        out_weight,
        out_bias,
        attn_gain,
        attn_shift,
        up_weight,
        up_bias,
        down_weight,
        down_bias,
        ffn_gain,
        ffn_shift,
    )
    gathered = (
        lax.all_gather(params[0], "dp", axis=0, tiled=True),
        lax.all_gather(params[1], "dp", axis=0, tiled=True),
        lax.all_gather(params[2], "dp", axis=0, tiled=True),
        lax.all_gather(params[3], "dp", axis=0, tiled=True),
        lax.all_gather(params[4], "dp", axis=0, tiled=True),
        lax.all_gather(params[5], "dp", axis=0, tiled=True),
        lax.all_gather(params[6], "dp", axis=0, tiled=True),
        lax.all_gather(params[7], "dp", axis=0, tiled=True),
        lax.all_gather(params[8], "dp", axis=0, tiled=True),
        lax.all_gather(params[9], "dp", axis=0, tiled=True),
        lax.all_gather(params[10], "dp", axis=0, tiled=True),
        lax.all_gather(params[11], "dp", axis=0, tiled=True),
        lax.all_gather(params[12], "dp", axis=0, tiled=True),
    )
    (
        w_qkv,
        q_bias,
        v_bias,
        w_out,
        b_out,
        gain_raw,
        shift_raw,
        w_up,
        b_up,
        w_down,
        b_down,
        gain_last,
        shift_last,
    ) = gathered
    seqs_here, block, width_model = layer_in.shape
    full_len = block * lax.axis_size("seq")
    rows = seqs_here * block
    pair_width = 2 * HD
    pair_count = H // 2
    score_scale = HD ** (-0.5)
    bias_qkv = jnp.concatenate(
        [q_bias.astype(jnp.float32), jnp.zeros((D,), jnp.float32), v_bias.astype(jnp.float32)]
    )
    gain_one = gain_raw.astype(jnp.float32)
    shift_one = shift_raw.astype(jnp.float32)
    gain_two = gain_last.astype(jnp.float32)
    shift_two = shift_last.astype(jnp.float32)
    tokens = layer_in.reshape(rows, D)
    qkv_proj = (jnp.dot(tokens, w_qkv, preferred_element_type=jnp.float32) + bias_qkv).astype(
        jnp.bfloat16
    )
    qkv_proj = qkv_proj.reshape(seqs_here, block, 3 * D)
    queries = qkv_proj[:, :, :D]
    keys_here = qkv_proj[:, :, D : 2 * D]
    values_here = qkv_proj[:, :, 2 * D :]
    keys_all, values_all = (
        lax.all_gather(keys_here, "seq", axis=1, tiled=True),
        lax.all_gather(values_here, "seq", axis=1, tiled=True),
    )
    valid = jnp.arange(full_len)[None, :] < lengths[:, None]

    def pair_part(array, pair_idx):
        piece = lax.dynamic_slice_in_dim(array, pair_idx * pair_width, pair_width, 2)
        return piece.reshape(piece.shape[:2] + (2, HD))

    def pair_scores(query_pair, key_pair):
        scores = (
            jnp.einsum("sbhd,slhd->shbl", query_pair, key_pair, preferred_element_type=jnp.float32)
            * score_scale
        )
        return jnp.where(valid[:, None, None, :], scores, mask_fill)

    def forward_pair(pair_idx):
        query_pair = pair_part(queries, pair_idx)
        key_pair = pair_part(keys_all, pair_idx)
        value_pair = pair_part(values_all, pair_idx)
        scores = pair_scores(query_pair, key_pair)
        row_top = jnp.max(scores, axis=-1, keepdims=True)
        log_sum = row_top + jnp.log(jnp.sum(jnp.exp(scores - row_top), axis=-1, keepdims=True))
        probs = jnp.exp(scores - log_sum).astype(jnp.bfloat16)
        mixed = jnp.einsum("shbl,slhd->sbhd", probs, value_pair, preferred_element_type=jnp.float32)
        return (mixed.astype(jnp.bfloat16).reshape(seqs_here, block, pair_width), log_sum)

    pair_out, log_sums = lax.map(forward_pair, jnp.arange(pair_count))

    def heads_side(stacked):
        return jnp.transpose(stacked, (1, 2, 0, 3)).reshape(rows, D)

    attended = heads_side(pair_out)
    first_sum = (
        tokens.astype(jnp.float32)
        + jnp.dot(attended, w_out, preferred_element_type=jnp.float32)
        + b_out.astype(jnp.float32)
    )
    first_norm, normed_one, inverse_one = layer_norm(first_sum, gain_one, shift_one)
    first_round = first_norm.astype(jnp.bfloat16)
    inner = jnp.dot(first_round, w_up, preferred_element_type=jnp.float32) + b_up.astype(
        jnp.float32
    )
    activated = gelu_exact(inner).astype(jnp.bfloat16)
    second_sum = (
        first_norm
        + jnp.dot(activated, w_down, preferred_element_type=jnp.float32)
        + b_down.astype(jnp.float32)
    )
    layer_out, normed_two, inverse_two = layer_norm(second_sum, gain_two, shift_two)
    (
        w_qkv,
        q_bias,
        v_bias,
        w_out,
        b_out,
        gain_raw,
        shift_raw,
        w_up,
        b_up,
        w_down,
        b_down,
        gain_last,
        shift_last,
    ) = (
        lax.all_gather(params[0], "dp", axis=0, tiled=True),
        lax.all_gather(params[1], "dp", axis=0, tiled=True),
        lax.all_gather(params[2], "dp", axis=0, tiled=True),
        lax.all_gather(params[3], "dp", axis=0, tiled=True),
        lax.all_gather(params[4], "dp", axis=0, tiled=True),
        lax.all_gather(params[5], "dp", axis=0, tiled=True),
        lax.all_gather(params[6], "dp", axis=0, tiled=True),
        lax.all_gather(params[7], "dp", axis=0, tiled=True),
        lax.all_gather(params[8], "dp", axis=0, tiled=True),
        lax.all_gather(params[9], "dp", axis=0, tiled=True),
        lax.all_gather(params[10], "dp", axis=0, tiled=True),
        lax.all_gather(params[11], "dp", axis=0, tiled=True),
        lax.all_gather(params[12], "dp", axis=0, tiled=True),
    )
    gain_one = gain_raw.astype(jnp.float32)
    gain_two = gain_last.astype(jnp.float32)
    upstream = grad_out.reshape(rows, D).astype(jnp.float32)
    ffn_gain_grad = jnp.sum(upstream * normed_two, axis=0)
    ffn_shift_grad = jnp.sum(upstream, axis=0)
    d_second = norm_back(upstream, normed_two, inverse_two, gain_two)
    d_second_round = d_second.astype(jnp.bfloat16)
    down_weight_grad = jnp.dot(activated.T, d_second_round, preferred_element_type=jnp.float32)
    down_bias_grad = jnp.sum(d_second, axis=0)
    d_inner = jnp.dot(d_second_round, w_down.T, preferred_element_type=jnp.float32) * gelu_slope(
        inner
    )
    d_inner_round = d_inner.astype(jnp.bfloat16)
    up_weight_grad = jnp.dot(first_round.T, d_inner_round, preferred_element_type=jnp.float32)
    up_bias_grad = jnp.sum(d_inner, axis=0)
    d_first_norm = d_second + jnp.dot(d_inner_round, w_up.T, preferred_element_type=jnp.float32)
    attn_gain_grad = jnp.sum(d_first_norm * normed_one, axis=0)
    attn_shift_grad = jnp.sum(d_first_norm, axis=0)
    d_first = norm_back(d_first_norm, normed_one, inverse_one, gain_one)
    d_first_round = d_first.astype(jnp.bfloat16)
    out_weight_grad = jnp.dot(attended.T, d_first_round, preferred_element_type=jnp.float32)
    out_bias_grad = jnp.sum(d_first, axis=0)
    d_attended = jnp.dot(d_first_round, w_out.T, preferred_element_type=jnp.float32).astype(
        jnp.bfloat16
    )
    d_attended = d_attended.reshape(seqs_here, block, D)

    def backward_pair(item):
        pair_idx, log_sum = item
        query_pair = pair_part(queries, pair_idx)
        key_pair = pair_part(keys_all, pair_idx)
        value_pair = pair_part(values_all, pair_idx)
        grad_pair = pair_part(d_attended, pair_idx)
        probs_exact = jnp.exp(pair_scores(query_pair, key_pair) - log_sum)
        d_probs = jnp.einsum(
            "sbhd,slhd->shbl", grad_pair, value_pair, preferred_element_type=jnp.float32
        )
        row_dot = jnp.sum(probs_exact * d_probs, axis=-1, keepdims=True)
        d_scores = (probs_exact * (d_probs - row_dot) * score_scale).astype(jnp.bfloat16)
        probs = probs_exact.astype(jnp.bfloat16)
        d_query = jnp.einsum(
            "shbl,slhd->sbhd", d_scores, key_pair, preferred_element_type=jnp.float32
        )
        d_key = jnp.einsum(
            "shbl,sbhd->slhd", d_scores, query_pair, preferred_element_type=jnp.float32
        )
        d_value = jnp.einsum(
            "shbl,sbhd->slhd", probs, grad_pair, preferred_element_type=jnp.float32
        )
        return (
            d_query.reshape(seqs_here, block, pair_width),
            d_key.reshape(seqs_here, full_len, pair_width),
            d_value.reshape(seqs_here, full_len, pair_width),
        )

    query_pairs, key_pairs, value_pairs = lax.map(backward_pair, (jnp.arange(pair_count), log_sums))
    key_pairs, value_pairs = (
        lax.psum_scatter(key_pairs, "seq", scatter_dimension=2, tiled=True),
        lax.psum_scatter(value_pairs, "seq", scatter_dimension=2, tiled=True),
    )
    d_query = heads_side(query_pairs)
    d_key = heads_side(key_pairs)
    d_value = heads_side(value_pairs)
    d_qkv = jnp.concatenate([d_query, d_key, d_value], axis=1).astype(jnp.bfloat16)
    qkv_weight_grad = jnp.dot(tokens.T, d_qkv, preferred_element_type=jnp.float32)
    query_bias_grad = jnp.sum(d_query, axis=0)
    value_bias_grad = jnp.sum(d_value, axis=0)
    grad_in = d_first + jnp.dot(d_qkv, w_qkv.T, preferred_element_type=jnp.float32)
    grads = (
        qkv_weight_grad,
        query_bias_grad,
        value_bias_grad,
        out_weight_grad,
        out_bias_grad,
        attn_gain_grad,
        attn_shift_grad,
        up_weight_grad,
        up_bias_grad,
        down_weight_grad,
        down_bias_grad,
        ffn_gain_grad,
        ffn_shift_grad,
    )
    owned = (
        lax.psum_scatter(grads[0], "dp", scatter_dimension=0, tiled=True),
        lax.psum_scatter(grads[1], "dp", scatter_dimension=0, tiled=True),
        lax.psum_scatter(grads[2], "dp", scatter_dimension=0, tiled=True),
        lax.psum_scatter(grads[3], "dp", scatter_dimension=0, tiled=True),
        lax.psum_scatter(grads[4], "dp", scatter_dimension=0, tiled=True),
        lax.psum_scatter(grads[5], "dp", scatter_dimension=0, tiled=True),
        lax.psum_scatter(grads[6], "dp", scatter_dimension=0, tiled=True),
        lax.psum_scatter(grads[7], "dp", scatter_dimension=0, tiled=True),
        lax.psum_scatter(grads[8], "dp", scatter_dimension=0, tiled=True),
        lax.psum_scatter(grads[9], "dp", scatter_dimension=0, tiled=True),
        lax.psum_scatter(grads[10], "dp", scatter_dimension=0, tiled=True),
        lax.psum_scatter(grads[11], "dp", scatter_dimension=0, tiled=True),
        lax.psum_scatter(grads[12], "dp", scatter_dimension=0, tiled=True),
    )
    owned = lax.psum(
        (
            owned[0],
            owned[1],
            owned[2],
            owned[3],
            owned[4],
            owned[5],
            owned[6],
            owned[7],
            owned[8],
            owned[9],
            owned[10],
            owned[11],
            owned[12],
        ),
        "seq",
    )
    return (layer_out.reshape(seqs_here, block, D), grad_in.reshape(seqs_here, block, D)) + tuple(
        owned
    )


def split_fits(mesh, heads, width, hidden):
    dp, seq = mesh.shape["dp"], mesh.shape["seq"]
    return heads % seq == 0 and dp % 2 == 0 and width % (dp * seq) == 0 and hidden % (dp * seq) == 0


def remote(src, dst, send_sem, recv_sem, peer):
    copy = pltpu.make_async_remote_copy(
        src_ref=src,
        dst_ref=dst,
        send_sem=send_sem,
        recv_sem=recv_sem,
        device_id=peer,
        device_id_type=pl.DeviceIdType.MESH,
    )
    copy.start()
    return copy


def greet(peers):
    barrier = pltpu.get_barrier_semaphore()
    for peer in peers:
        pl.semaphore_signal(
            barrier, inc=1, device_id=peer, device_id_type=pl.DeviceIdType.MESH
        )
    pl.semaphore_wait(barrier, len(peers))


def places(owners, parts):
    at = lax.axis_index("dp")
    line, side = at // 2, at % 2
    lines = owners // 2
    me = lax.axis_index("seq")
    line_peers = [{"dp": ((line + k) % lines) * 2 + side} for k in range(1, lines)]
    seq_peers = [{"seq": (me + k) % parts} for k in range(1, parts)]
    return line, side, lines, me, line_peers, {"dp": line * 2 + 1 - side}, seq_peers


def start_kernel(
    owners, parts, x_ref, w_ref, x_out, w_out, x_send, x_recv, l_send, l_recv, p_send, p_recv
):
    line, side, lines, me, line_peers, pair, seq_peers = places(owners, parts)
    greet(line_peers + [pair] + seq_peers)
    block = x_ref.shape[1]
    mine = line * 2 + side
    rows = pl.ds(pl.multiple_of(me * block, block), block)
    copies = []
    for k, peer in enumerate(line_peers):
        copies.append(remote(w_ref, w_out.at[mine], l_send.at[k], l_recv.at[k], peer))
    paired = [remote(w_ref, w_out.at[mine], p_send.at[0], p_recv.at[0], pair)]
    tokens = []
    for k, peer in enumerate(seq_peers):
        tokens.append(remote(x_ref, x_out.at[:, rows, :], x_send.at[k], x_recv.at[k], peer))
    w_out[mine] = w_ref[...]
    x_out[:, rows, :] = x_ref[...]
    for k in range(1, lines):
        copies[k - 1].wait_recv()
        slot = w_out.at[((line + lines - k) % lines) * 2 + side]
        paired.append(remote(slot, slot, p_send.at[k], p_recv.at[k], pair))
    for copy in copies:
        copy.wait_send()
    for copy in paired + tokens:
        copy.wait()


def gather_start(layer_in, weights, owners, parts):
    seqs_here, block, width = layer_in.shape
    own, cols = weights.shape
    vmem = pl.BlockSpec(memory_space=pltpu.VMEM)
    dma = pltpu.SemaphoreType.DMA
    lines = owners // 2
    return pl.pallas_call(
        functools.partial(start_kernel, owners, parts),
        out_shape=(
            jax.ShapeDtypeStruct((seqs_here, block * parts, width), layer_in.dtype),
            jax.ShapeDtypeStruct((owners, own, cols), weights.dtype),
        ),
        in_specs=[vmem, vmem],
        out_specs=(vmem, vmem),
        scratch_shapes=[
            dma((parts - 1,)),
            dma((parts - 1,)),
            dma((lines - 1,)),
            dma((lines - 1,)),
            dma((lines,)),
            dma((lines,)),
        ],
        compiler_params=pltpu.CompilerParams(collective_id=0, has_side_effects=True),
        cost_estimate=pl.CostEstimate(flops=0, bytes_accessed=80_000_000, transcendentals=0),
    )(layer_in, weights)


def end_kernel(
    owners,
    parts,
    g_ref,
    d_ref,
    g_out,
    d_out,
    pair_in,
    line_out,
    line_in,
    total,
    d_send,
    d_recv,
    p_send,
    p_recv,
    l_send,
    l_recv,
    s_send,
    s_recv,
):
    line, side, lines, me, line_peers, pair, seq_peers = places(owners, parts)
    greet(line_peers + [pair] + seq_peers)
    block = d_ref.shape[1] // parts
    order = list(range(1, lines)) + [0]
    paired = {}
    for k in order:
        owner = ((line + k) % lines) * 2
        paired[k] = remote(
            g_ref.at[owner + 1 - side], pair_in.at[k], p_send.at[k], p_recv.at[k], pair
        )
    inputs = []
    for k, peer in enumerate(seq_peers):
        start = pl.multiple_of(((me + k + 1) % parts) * block, block)
        piece = d_ref.at[:, pl.ds(start, block), :]
        inputs.append(remote(piece, d_out.at[k], d_send.at[k], d_recv.at[k], peer))
    lined = []
    for k in range(1, lines):
        paired[k].wait_recv()
        owner = ((line + k) % lines) * 2
        both = g_ref[owner + side].astype(jnp.float32) + pair_in[k].astype(jnp.float32)
        line_out[k - 1] = both.astype(line_out.dtype)
        lined.append(
            remote(
                line_out.at[k - 1],
                line_in.at[k - 1],
                l_send.at[k - 1],
                l_recv.at[k - 1],
                line_peers[k - 1],
            )
        )
    paired[0].wait_recv()
    held = g_ref[line * 2 + side].astype(jnp.float32) + pair_in[0].astype(jnp.float32)
    for k in range(1, lines):
        lined[k - 1].wait_recv()
        held = held + line_in[k - 1].astype(jnp.float32)
    total[...] = held.astype(total.dtype)
    g_out[me] = held.astype(g_out.dtype)
    shared = []
    for k, peer in enumerate(seq_peers):
        shared.append(remote(total, g_out.at[me], s_send.at[k], s_recv.at[k], peer))
    for k in range(lines):
        paired[k].wait_send()
    for copy in lined:
        copy.wait_send()
    for copy in inputs + shared:
        copy.wait()


def scatter_end(grads, partial, owners, parts):
    rows, cols = grads.shape
    own, lines = rows // owners, owners // 2
    seqs_here, full_len, width = partial.shape
    block = full_len // parts
    vmem = pl.BlockSpec(memory_space=pltpu.VMEM)
    dma = pltpu.SemaphoreType.DMA
    dtype = grads.dtype
    return pl.pallas_call(
        functools.partial(end_kernel, owners, parts),
        out_shape=(
            jax.ShapeDtypeStruct((parts, own, cols), dtype),
            jax.ShapeDtypeStruct((parts - 1, seqs_here, block, width), partial.dtype),
        ),
        in_specs=[vmem, vmem],
        out_specs=(vmem, vmem),
        scratch_shapes=[
            pltpu.VMEM((lines, own, cols), dtype),
            pltpu.VMEM((lines - 1, own, cols), dtype),
            pltpu.VMEM((lines - 1, own, cols), dtype),
            pltpu.VMEM((own, cols), dtype),
            dma((parts - 1,)),
            dma((parts - 1,)),
            dma((lines,)),
            dma((lines,)),
            dma((lines - 1,)),
            dma((lines - 1,)),
            dma((parts - 1,)),
            dma((parts - 1,)),
        ],
        compiler_params=pltpu.CompilerParams(collective_id=1, has_side_effects=True),
        cost_estimate=pl.CostEstimate(flops=0, bytes_accessed=80_000_000, transcendentals=0),
    )(grads.reshape(owners, own, cols), partial)


def seq_kernel(parts, kind, x_ref, out_ref, send, recv):
    me = lax.axis_index("seq")
    peers = [{"seq": (me + k) % parts} for k in range(1, parts)]
    greet(peers)
    copies = []
    if kind == "deal":
        block = x_ref.shape[1] // parts
        for k, peer in enumerate(peers):
            start = pl.multiple_of(((me + k + 1) % parts) * block, block)
            piece = x_ref.at[:, pl.ds(start, block), :]
            copies.append(remote(piece, out_ref.at[k], send.at[k], recv.at[k], peer))
    else:
        block = x_ref.shape[1]
        if kind == "rows":
            slot = (slice(None), pl.ds(pl.multiple_of(me * block, block), block))
        else:
            slot = (me,)
        for k, peer in enumerate(peers):
            copies.append(remote(x_ref, out_ref.at[slot], send.at[k], recv.at[k], peer))
        out_ref[slot] = x_ref[...]
    for copy in copies:
        copy.wait()


def seq_call(array, parts, kind, number):
    seqs_here, rows, width = array.shape
    if kind == "deal":
        shape = (parts - 1, seqs_here, rows // parts, width)
    elif kind == "rows":
        shape = (seqs_here, rows * parts, width)
    else:
        shape = (parts, seqs_here, rows, width)
    vmem = pl.BlockSpec(memory_space=pltpu.VMEM)
    dma = pltpu.SemaphoreType.DMA
    return pl.pallas_call(
        functools.partial(seq_kernel, parts, kind),
        out_shape=jax.ShapeDtypeStruct(shape, array.dtype),
        in_specs=[vmem],
        out_specs=vmem,
        scratch_shapes=[dma((parts - 1,)), dma((parts - 1,))],
        compiler_params=pltpu.CompilerParams(collective_id=number, has_side_effects=True),
        cost_estimate=pl.CostEstimate(flops=0, bytes_accessed=15_000_000, transcendentals=0),
    )(array)


def scatter_dp(grads):
    return lax.psum_scatter(grads.astype(jnp.bfloat16), "dp", scatter_dimension=0, tiled=True)


def on_device(
    layer_in,
    lengths,
    qkv_weight,
    query_bias,
    value_bias,
    out_weight,
    out_bias,
    attn_gain,
    attn_shift,
    up_weight,
    up_bias,
    down_weight,
    down_bias,
    ffn_gain,
    ffn_shift,
    grad_out,
):
    f32, bf16 = jnp.float32, jnp.bfloat16
    parts, me = lax.axis_size("seq"), lax.axis_index("seq")
    owners = lax.axis_size("dp")
    seqs_here, block, width = layer_in.shape
    full_len = block * parts
    own = qkv_weight.shape[0]
    heads = H // parts
    cols = heads * HD
    hidden = up_weight.shape[1]
    unit = hidden // (owners * parts)
    hidden_part = owners * unit
    score_scale = HD ** (-0.5)

    def dot(a, b):
        return jnp.dot(a, b, preferred_element_type=f32)

    def flat(array):
        return array.reshape(-1, array.shape[-1])

    qkv_mine = lax.dynamic_index_in_dim(
        qkv_weight.reshape(own, 3, parts, cols), me, 2, keepdims=False
    ).reshape(own, 3 * cols)
    up_mine = lax.dynamic_index_in_dim(
        up_weight.reshape(own, owners, parts, unit), me, 2, keepdims=False
    ).reshape(own, hidden_part)
    down_mine = lax.dynamic_slice_in_dim(down_weight, me * unit, unit, 0)
    up_bias_mine = lax.dynamic_slice_in_dim(up_bias, me * unit, unit, 0)
    small = jnp.stack(
        [
            query_bias,
            value_bias,
            out_bias,
            attn_gain,
            attn_shift,
            down_bias,
            ffn_gain,
            ffn_shift,
            up_bias_mine,
        ],
        axis=1,
    )
    small = jnp.pad(small, ((0, 0), (0, 128 - small.shape[1])))
    tokens, early = gather_start(
        layer_in, jnp.concatenate([out_weight, small, qkv_mine], axis=1), owners, parts
    )
    early = flat(early)
    late = lax.all_gather(
        jnp.concatenate([up_mine, down_mine], axis=1), "dp", axis=0, tiled=True
    )
    w_out = early[:, :width]
    vectors = early[:, width : width + 128].T.astype(f32)
    w_qkv = early[:, width + 128 :]
    w_up = late[:, :hidden_part]
    w_down = late[:, hidden_part:]
    q_bias, v_bias, b_out, gain_one, shift_one, b_down, gain_two, shift_two, b_up = [
        vectors[k] for k in range(9)
    ]

    def mine(vector):
        return lax.dynamic_slice_in_dim(vector, me * cols, cols, 0)

    bias_qkv = jnp.concatenate([mine(q_bias), jnp.zeros((cols,), f32), mine(v_bias)])
    tokens_flat = flat(tokens)
    qkv = (dot(tokens_flat, w_qkv) + bias_qkv).astype(bf16)
    qkv = qkv.reshape(seqs_here, full_len, 3, heads, HD).transpose(2, 0, 3, 1, 4)
    queries, keys, values = qkv[0], qkv[1], qkv[2]
    valid = jnp.arange(full_len)[None, :] < lengths[:, None]
    scores = jnp.einsum("shbd,shld->shbl", queries, keys, preferred_element_type=f32)
    scores = jnp.where(valid[:, None, None, :], scores * score_scale, mask_fill)
    row_top = jnp.max(scores, axis=-1, keepdims=True)
    log_sum = row_top + jnp.log(jnp.sum(jnp.exp(scores - row_top), axis=-1, keepdims=True))
    probs_exact = jnp.exp(scores - log_sum)
    probs = probs_exact.astype(bf16)
    mixed = jnp.einsum("shbl,shld->shbd", probs, values, preferred_element_type=f32)
    mixed = mixed.astype(bf16).transpose(0, 2, 1, 3).reshape(seqs_here, full_len, cols)
    attended = seq_call(mixed, parts, "slots", 2)
    attended_flat = attended.transpose(1, 2, 0, 3).reshape(seqs_here * full_len, width)
    first_sum = tokens_flat.astype(f32) + dot(attended_flat, w_out) + b_out
    first_norm, normed_all, inverse_all = layer_norm(first_sum, gain_one, shift_one)

    def here(rows):
        rows = rows.reshape(seqs_here, full_len, rows.shape[-1])
        return flat(lax.dynamic_slice_in_dim(rows, me * block, block, 1))

    normed_one, inverse_one = here(normed_all), here(inverse_all)
    first_round = first_norm.astype(bf16)

    def deal(partial, number):
        pieces = partial.astype(bf16).reshape(seqs_here, full_len, width)
        others = seq_call(pieces, parts, "deal", number)
        return here(partial) + flat(jnp.sum(others.astype(f32), axis=0))

    inner = dot(first_round, w_up) + b_up
    activated = gelu_exact(inner).astype(bf16)
    down = deal(dot(activated, w_down), 3)
    second_sum = here(first_norm) + down + b_down
    layer_out, normed_two, inverse_two = layer_norm(second_sum, gain_two, shift_two)

    upstream = flat(grad_out).astype(f32)
    ffn_gain_grad = jnp.sum(upstream * normed_two, axis=0)
    ffn_shift_grad = jnp.sum(upstream, axis=0)
    d_second = norm_back(upstream, normed_two, inverse_two, gain_two)
    d_second_all = flat(
        seq_call(d_second.astype(bf16).reshape(seqs_here, block, width), parts, "rows", 4)
    )
    down_bias_grad = jnp.sum(d_second, axis=0)
    d_inner = dot(d_second_all, w_down.T) * gelu_slope(inner)
    d_inner_round = d_inner.astype(bf16)
    d_up = deal(dot(d_inner_round, w_up.T), 5)
    down_weight_grad = dot(activated.T, d_second_all)
    up_weight_grad = dot(first_round.T, d_inner_round)
    up_bias_grad = jnp.sum(d_inner, axis=0)
    late_grads = scatter_dp(up_weight_grad)
    d_first_norm = d_second + d_up
    attn_gain_grad = jnp.sum(d_first_norm * normed_one, axis=0)
    attn_shift_grad = jnp.sum(d_first_norm, axis=0)
    d_first = norm_back(d_first_norm, normed_one, inverse_one, gain_one)
    out_bias_grad = jnp.sum(d_first, axis=0)
    d_first_all = flat(
        seq_call(d_first.astype(bf16).reshape(seqs_here, block, width), parts, "rows", 6)
    )
    out_weight_grad = dot(
        attended_flat.T, lax.dynamic_slice_in_dim(d_first_all, me * cols, cols, 1)
    )
    w_out_mine = lax.dynamic_slice_in_dim(w_out, me * cols, cols, 0)
    d_attended = dot(d_first_all, w_out_mine.T).astype(bf16)
    d_attended = d_attended.reshape(seqs_here, full_len, heads, HD).transpose(0, 2, 1, 3)
    d_probs = jnp.einsum("shbd,shld->shbl", d_attended, values, preferred_element_type=f32)
    row_dot = jnp.sum(probs_exact * d_probs, axis=-1, keepdims=True)
    d_scores = (probs_exact * (d_probs - row_dot) * score_scale).astype(bf16)
    d_query = jnp.einsum("shbl,shld->shbd", d_scores, keys, preferred_element_type=f32)
    d_key = jnp.einsum("shbl,shbd->shld", d_scores, queries, preferred_element_type=f32)
    d_value = jnp.einsum("shbl,shbd->shld", probs, d_attended, preferred_element_type=f32)
    query_bias_grad = jnp.sum(d_query, axis=(0, 2)).reshape(cols)
    value_bias_grad = jnp.sum(d_value, axis=(0, 2)).reshape(cols)
    d_qkv = jnp.stack([d_query, d_key, d_value]).astype(bf16)
    d_qkv = d_qkv.transpose(1, 3, 0, 2, 4).reshape(seqs_here * full_len, 3 * cols)
    qkv_weight_grad = dot(tokens_flat.T, d_qkv)

    def placed(vector):
        return lax.dynamic_update_slice_in_dim(jnp.zeros((width,), f32), vector, me * cols, 0)

    small_grads = jnp.stack(
        [
            placed(query_bias_grad),
            placed(value_bias_grad),
            out_bias_grad,
            attn_gain_grad,
            attn_shift_grad,
            down_bias_grad,
            ffn_gain_grad,
            ffn_shift_grad,
            up_bias_grad,
        ]
    )
    small_grads = jnp.pad(small_grads, ((0, 128 - small_grads.shape[0]), (0, 0))).T
    d_in = dot(d_qkv, w_qkv.T)
    early_all, d_others = scatter_end(
        jnp.concatenate(
            [down_weight_grad, small_grads, qkv_weight_grad, out_weight_grad], axis=1
        ).astype(bf16),
        d_in.reshape(seqs_here, full_len, width).astype(bf16),
        owners,
        parts,
    )
    grad_in = d_first + here(d_in) + flat(jnp.sum(d_others.astype(f32), axis=0))

    late_all = lax.all_gather(late_grads, "seq", axis=0)
    down_owned = early_all[:, :, :width].reshape(parts * unit, width).astype(f32)
    early_all = early_all[:, :, width:]
    up_owned = late_all.reshape(parts, own, owners, unit)
    up_owned = up_owned.transpose(1, 2, 0, 3).reshape(own, hidden).astype(f32)
    small_owned = early_all[:, :, :128].astype(f32)
    sums = jnp.sum(small_owned, axis=0).T
    up_bias_owned = small_owned[:, :, 8].reshape(parts * unit)
    qkv_owned = early_all[:, :, 128 : 128 + 3 * cols].reshape(parts, own, 3, cols)
    qkv_owned = qkv_owned.transpose(1, 2, 0, 3).reshape(own, 3 * width).astype(f32)
    out_owned = early_all[:, :, 128 + 3 * cols :].transpose(1, 0, 2).reshape(own, width)
    return (
        layer_out.reshape(seqs_here, block, width),
        grad_in.reshape(seqs_here, block, width),
        qkv_owned,
        sums[0],
        sums[1],
        out_owned.astype(f32),
        sums[2],
        sums[3],
        sums[4],
        up_owned,
        up_bias_owned,
        down_owned,
        sums[5],
        sums[6],
        sums[7],
    )


def solution(mesh):
    in_specs = (
        P("dp", "seq", None),
        P("dp"),
        P("dp", None),
        P("dp"),
        P("dp"),
        P("dp", None),
        P("dp"),
        P("dp"),
        P("dp"),
        P("dp", None),
        P("dp"),
        P("dp", None),
        P("dp"),
        P("dp"),
        P("dp"),
        P("dp", "seq", None),
    )
    out_specs = (
        P("dp", "seq", None),
        P("dp", "seq", None),
        P("dp", None),
        P("dp"),
        P("dp"),
        P("dp", None),
        P("dp"),
        P("dp"),
        P("dp"),
        P("dp", None),
        P("dp"),
        P("dp", None),
        P("dp"),
        P("dp"),
        P("dp"),
    )
    body = on_device if split_fits(mesh, H, D, FF) else on_device_general
    return jax.shard_map(
        body, mesh=mesh, in_specs=in_specs, out_specs=out_specs, check_vma=False
    )
```
